512 devices in a mesh: dp: 16 (over x, y), blk: 32 (over z, core).
Axes of the slice: x: 4, y: 4, z: 16, core: 2. Of those that a mesh axis runs over, the one named last changes fastest.
Arguments:
- tokens: bfloat16 [4096, 8192], P('dp', 'blk'), may hold values from -6 to 6
- up_blocks: bfloat16 [32, 80, 128, 128], P('blk'), may hold values from -0.125 to 0.125
- block_list: int32 [32, 80, 2], P('blk'), may hold values from -1 to 63, as said below
- row_cut: int32 [32, 2], replicated, may hold values from 0 to 63, as said below
- out_grad: bfloat16 [4096, 16384], P('dp', 'blk'), may hold values from -6 to 6
Outputs:
- activated: bfloat16 [4096, 16384], P('dp', 'blk')
- in_grad: bfloat16 [4096, 8192], P('dp', 'blk')
- block_grad: float32 [32, 80, 128, 128], P('blk', 'dp')
The draws below stay inside these ranges and needn't reach their ends.
Inputs may be any that keep to these rules, and one draw needn't show every extreme that they name: In each block_list[j] the used slots name distinct blocks with a block row below 64 and a column slot below 4; an unused slot holds -1 in both entries, anywhere in the list; every index j uses at least 48 slots and some j uses all 80. Every block row appears exactly once in row_cut.
All inputs are finite; a program needn't handle non-finite values.
Results may differ from the reference program's by a relative error of at most 0.015.
Values may be sent and summed in bfloat16 or wider, within the bound.
No kernel may reach another device: no remote copies, remote signals or barrier semaphores. Data moves between devices by JAX's collectives and lax.ppermute only.
A program may use at most 128 MiB of HBM per device.

```python
import jax
import jax.numpy as jnp
from jax import lax

D = 8192
F = 16384
B = 128
KD = 64
KF = 128
COLS = 4
ROWS = 2
CAP = 80
TOKENS = 4096
N_DP = 16
N_BLK = 32


def block_layout(key):
    key_list = jax.random.split(jax.random.fold_in(key, 7), 7)
    dev_total = KF // COLS
    cell_count = KD * COLS
    row_bias = jax.random.randint(key_list[0], (KD,), 0, 4)
    col_bias = jax.random.randint(key_list[1], (dev_total, COLS), 0, 4)
    jitter = jax.random.randint(key_list[2], (dev_total, cell_count), 0, 1024)
    cell_ids = jnp.arange(cell_count, dtype=jnp.int32)
    cell_bias = row_bias[cell_ids // COLS][None, :] + col_bias[:, cell_ids % COLS]
    cell_score = (cell_bias * 1024 + jitter) * cell_count + cell_ids[None, :]
    top_score, top_cell = lax.top_k(cell_score, CAP)
    used_count = jax.random.randint(key_list[3], (dev_total,), 3 * CAP // 5, CAP + 1)
    full_dev = jax.random.randint(key_list[4], (), 0, dev_total)
    used_count = jnp.where(jnp.arange(dev_total) == full_dev, CAP, used_count)
    is_live = jnp.arange(CAP)[None, :] < used_count[:, None]
    slot_order = jax.vmap(lambda sub_key: jax.random.permutation(sub_key, CAP))(jax.random.split(key_list[5], dev_total))
    top_cell = jnp.take_along_axis(top_cell, slot_order, axis=1)
    is_live = jnp.take_along_axis(is_live, slot_order, axis=1)
    block_rows = jnp.where(is_live, top_cell // COLS, -1)
    block_cols = jnp.where(is_live, top_cell % COLS, -1)
    listed = jnp.stack([block_rows, block_cols], axis=-1).astype(jnp.int32)
    row_hits = (block_rows[:, :, None] == jnp.arange(KD, dtype=jnp.int32)[None, None, :]).astype(jnp.int32)
    row_load = jnp.sum(row_hits, axis=(0, 1))
    tie_break = jax.random.permutation(key_list[6], KD)
    sorted_rows = jnp.argsort(-(row_load * KD + tie_break), stable=True).astype(jnp.int32)
    positions = jnp.arange(KD, dtype=jnp.int32)
    round_idx = positions // dev_total
    within = positions % dev_total
    target_dev = jnp.where(round_idx % 2 == 0, within, dev_total - 1 - within)
    row_cut = jnp.zeros((dev_total, ROWS), jnp.int32).at[target_dev, round_idx].set(sorted_rows)
    return (listed, row_cut)


def draw_block_list(key, part):
    listed, row_cut = block_layout(key)
    return listed


def draw_row_cut(key, part):
    listed, row_cut = block_layout(key)
    return row_cut


def level_of(stream_key, shape, shards, least, largest):
    def one(axis_at, blocks):
        draws = jax.random.uniform(jax.random.fold_in(jax.random.fold_in(stream_key, 6), axis_at), (blocks,), jnp.float32, least / len(shards), largest / len(shards))
        return jnp.repeat(jnp.exp(draws), shape[axis_at] // blocks).reshape((-1,) + (1,) * (len(shape) - axis_at - 1))

    gain = one(*shards[0])
    for cut in shards[1:]:
        gain = gain * one(*cut)
    return gain


def gaussian(key, dims, spread, limit, shards=(), kind=jnp.bfloat16):
    loudness = level_of(key, dims, shards, -0.22, 0.18) if shards else 1.0
    result = jax.random.normal(key, dims, jnp.float32) * spread * loudness
    return jnp.minimum(jnp.maximum(result, -limit), limit).astype(kind)


def setup_inputs(seed: int = 0) -> dict:
    seeds = jax.random.split(jax.random.key(seed), 6)
    tokens = gaussian(seeds[0], (TOKENS, D), 1.0, 6.0, ((0, 16), (1, 32)))
    up_blocks = gaussian(seeds[1], (N_BLK, CAP, B, B), (D // 4) ** -0.5, 0.125, ((0, 32),))
    block_list = draw_block_list(jax.random.fold_in(seeds[5], 71), 0)
    row_cut = draw_row_cut(jax.random.fold_in(seeds[5], 71), 0)
    out_grad = gaussian(seeds[4], (TOKENS, F), 1.0, 6.0, ((0, 16), (1, 32)))
    return {"tokens": tokens, "up_blocks": up_blocks, "block_list": block_list, "row_cut": row_cut, "out_grad": out_grad}


def reference(tokens, up_blocks, block_list, row_cut, out_grad):
    tok_count = tokens.shape[0]
    group_rows = tok_count // N_DP
    x_blocks = tokens.reshape(tok_count, KD, B)
    grad_cols = out_grad.reshape(tok_count, N_BLK, COLS, B)
    dest_rows = row_cut.reshape(-1).astype(jnp.int32)
    row_place = jnp.zeros((KD,), jnp.int32).at[dest_rows].set(jnp.arange(KD, dtype=jnp.int32))
    grad_scale = 1.0 / jnp.sqrt(jnp.float32(tok_count))

    def device_step(carry, index):
        weights = up_blocks[index].astype(jnp.float32)
        listed = block_list[index]
        block_rows = listed[:, 0]
        block_cols = listed[:, 1]
        is_used = block_rows >= 0
        safe_rows = jnp.maximum(block_rows, 0).astype(jnp.int32)
        safe_cols = jnp.maximum(block_cols, 0).astype(jnp.int32)
        col_pick = ((safe_cols[:, None] == jnp.arange(COLS, dtype=jnp.int32)[None, :]) & is_used[:, None]).astype(jnp.float32)
        picked = jnp.take(x_blocks, safe_rows, axis=1).astype(jnp.float32)
        per_slot = jnp.einsum('tsi,sio->sto', picked, weights)
        hidden = jnp.einsum('sto,sc->tco', per_slot, col_pick, precision=lax.Precision.HIGHEST)
        gate_sig = jax.nn.sigmoid(hidden)
        activated = (hidden * gate_sig).astype(jnp.bfloat16)
        pre_grad = (grad_cols[:, index].astype(jnp.float32) * gate_sig * (1.0 + hidden * (1.0 - gate_sig))).astype(jnp.bfloat16)
        col_grads = jnp.take(pre_grad, safe_cols, axis=1).astype(jnp.float32)
        slot_terms = jnp.einsum('tso,sio->sti', col_grads, weights)
        target = jnp.where(is_used, row_place[safe_rows], KD).astype(jnp.int32)
        partial_value = jax.ops.segment_sum(slot_terms, target, num_segments=KD).astype(jnp.bfloat16)
        group_terms = jnp.einsum('gtsi,gtso->gsio', picked.reshape(N_DP, group_rows, CAP, B), col_grads.reshape(N_DP, group_rows, CAP, B))
        rounded = lax.optimization_barrier(group_terms.astype(jnp.bfloat16))
        summed = lax.optimization_barrier(jnp.sum(rounded.astype(jnp.float32), axis=0))
        block_grad = summed * grad_scale * is_used.astype(jnp.float32)[:, None, None]
        return (carry + partial_value.astype(jnp.float32), (activated.reshape(tok_count, COLS * B), block_grad))
    start = jnp.zeros((KD, tok_count, B), jnp.float32)
    total, (act_parts, grad_parts) = lax.scan(device_step, start, jnp.arange(N_BLK, dtype=jnp.int32))
    activated = jnp.transpose(act_parts, (1, 0, 2)).reshape(tok_count, F)
    in_grad = jnp.transpose(total, (1, 0, 2)).reshape(tok_count, D).astype(jnp.bfloat16)
    return (activated, in_grad, grad_parts)
```

```python
import functools

import jax
import jax.numpy as jnp
from jax import lax
from jax.experimental import pallas as pl
from jax.experimental.pallas import tpu as pltpu
from jax.sharding import PartitionSpec as P

SMEM = pl.BlockSpec(memory_space=pltpu.SMEM)
VMEM = pl.BlockSpec(memory_space=pltpu.VMEM)
MIB = 1 << 20


def lay_weights(rows_per_dev, listed, cut, core, w_ref, up_ref, down_ref, place):
    half = cut.shape[0] // 2
    slots, blk = w_ref.shape[0], w_ref.shape[1]

    def note(p, carry):
        owner, a = p // rows_per_dev, p % rows_per_dev
        side = (owner % 2 != core[0]).astype(jnp.int32)
        place[cut[p]] = side * half + (owner // 2) * rows_per_dev + a
        return carry

    lax.fori_loop(0, cut.shape[0], note, 0)
    up_ref[...] = jnp.zeros_like(up_ref)
    down_ref[...] = jnp.zeros_like(down_ref)

    def put(s, carry):
        row, col = listed[2 * s], listed[2 * s + 1]

        @pl.when(row >= 0)
        def _():
            block = w_ref[s]
            dev, a = row // rows_per_dev, row % rows_per_dev
            up_ref[dev, pl.ds(pl.multiple_of(a * blk, blk), blk), pl.ds(pl.multiple_of(col * blk, blk), blk)] = block
            to = place[row]
            down_ref[to // rows_per_dev, pl.ds(pl.multiple_of(col * blk, blk), blk),
                     pl.ds(pl.multiple_of((to % rows_per_dev) * blk, blk), blk)] = block.T

        return carry

    lax.fori_loop(0, slots, put, 0)


def hidden_pass(x_ref, up_ref, down_ref, og_ref, act_ref, pg_ref, own_ref, other_ref, acc):
    devs = x_ref.shape[0]
    acc[...] = jnp.dot(x_ref[0], up_ref[0], preferred_element_type=jnp.float32)

    def add(b, carry):
        acc[...] += jnp.dot(x_ref[b], up_ref[b], preferred_element_type=jnp.float32)
        return carry

    lax.fori_loop(1, devs, add, 0)
    hidden = acc[...]
    sig = jax.nn.sigmoid(hidden)
    act_ref[...] = (hidden * sig).astype(jnp.bfloat16)
    pg_ref[...] = (og_ref[...].astype(jnp.float32) * sig * (1.0 + hidden * (1.0 - sig))).astype(jnp.bfloat16)
    half = devs // 2

    def back(k, carry):
        pg = pg_ref[...]
        own_ref[k] = jnp.dot(pg, down_ref[k], preferred_element_type=jnp.float32).astype(jnp.bfloat16)
        other_ref[k] = jnp.dot(pg, down_ref[half + k], preferred_element_type=jnp.float32).astype(jnp.bfloat16)
        return carry

    lax.fori_loop(0, half, back, 0)


def weight_terms(side, rows_per_dev, listed, at, x_ref, pg_ref, *out_refs):
    y_refs, x_refs = out_refs[:side], out_refs[side:]
    per, half, blk = y_refs[0].shape[1:]
    for dx in range(side):
        for dy in range(side):
            owner = lax.rem(at[0] + dx, side) * side + lax.rem(at[1] + dy, side)

            def one(q, carry, dx=dx, dy=dy, owner=owner):
                s = owner * per + q
                row, col = listed[2 * s], listed[2 * s + 1]

                @pl.when(row >= 0)
                def _():
                    dev, a = row // rows_per_dev, row % rows_per_dev
                    x = x_ref[dev, :, pl.ds(pl.multiple_of(a * blk, blk), blk)]
                    g = pg_ref[:, pl.ds(pl.multiple_of(col * blk, blk), blk)]
                    term = lax.dot_general(x, g, (((0,), (0,)), ((), ())), preferred_element_type=jnp.float32)
                    term = term.astype(jnp.bfloat16)
                    y_refs[dy][dx, q] = term[:half]
                    x_refs[dx][dy, q] = term[half:]

                @pl.when(row < 0)
                def _():
                    y_refs[dy][dx, q] = jnp.zeros((half, blk), jnp.bfloat16)
                    x_refs[dx][dy, q] = jnp.zeros((half, blk), jnp.bfloat16)

                return carry

            lax.fori_loop(0, per, one, 0)


def on_device(n_dp, n_blk, tokens, up_blocks, block_list, row_cut, out_grad):
    tok_rows, feats = tokens.shape
    slots, blk = up_blocks.shape[1], up_blocks.shape[2]
    width = out_grad.shape[1]
    rows_per_dev = row_cut.shape[1]
    side = 4
    bf16 = jnp.bfloat16
    z_groups = [list(range(c, n_blk, 2)) for c in range(2)]
    swap = [(i, i ^ 1) for i in range(n_blk)]
    listed = block_list.reshape(-1)
    cut = row_cut.reshape(-1)
    core = (lax.axis_index("blk") % 2).reshape(1).astype(jnp.int32)
    dp_at = lax.axis_index("dp")
    at = jnp.stack([dp_at // side, dp_at % side]).astype(jnp.int32)

    gathered = lax.all_gather(tokens, "blk", axis=0, tiled=False)

    up_w, down_w = pl.pallas_call(
        functools.partial(lay_weights, rows_per_dev),
        out_shape=(
            jax.ShapeDtypeStruct((n_blk, feats, width), bf16),
            jax.ShapeDtypeStruct((n_blk, width, feats), bf16),
        ),
        in_specs=[SMEM, SMEM, SMEM, VMEM],
        out_specs=(VMEM, VMEM),
        scratch_shapes=[pltpu.SMEM((cut.shape[0],), jnp.int32)],
        compiler_params=pltpu.CompilerParams(vmem_limit_bytes=24 * MIB),
        cost_estimate=pl.CostEstimate(flops=0, bytes_accessed=20 * MIB, transcendentals=0),
    )(listed, cut, core, up_blocks[0])

    act, pg, own, other = pl.pallas_call(
        hidden_pass,
        out_shape=(
            jax.ShapeDtypeStruct((tok_rows, width), bf16),
            jax.ShapeDtypeStruct((tok_rows, width), bf16),
            jax.ShapeDtypeStruct((n_blk // 2, tok_rows, feats), bf16),
            jax.ShapeDtypeStruct((n_blk // 2, tok_rows, feats), bf16),
        ),
        in_specs=[VMEM] * 4,
        out_specs=(VMEM,) * 4,
        scratch_shapes=[pltpu.VMEM((tok_rows, width), jnp.float32)],
        compiler_params=pltpu.CompilerParams(vmem_limit_bytes=32 * MIB),
        cost_estimate=pl.CostEstimate(
            flops=4 * tok_rows * width * n_blk * feats, bytes_accessed=24 * MIB, transcendentals=tok_rows * width
        ),
    )(gathered, up_w, down_w, out_grad)

    met = own.astype(jnp.float32) + lax.ppermute(other, "blk", swap).astype(jnp.float32)
    in_grad = lax.psum_scatter(
        met.astype(bf16), "blk", scatter_dimension=0, axis_index_groups=z_groups, tiled=True
    )[0]

    per = slots // n_dp
    piece = jax.ShapeDtypeStruct((side, per, blk // 2, blk), bf16)
    terms = pl.pallas_call(
        functools.partial(weight_terms, side, rows_per_dev),
        out_shape=(piece,) * (2 * side),
        in_specs=[SMEM, SMEM, VMEM, VMEM],
        out_specs=(VMEM,) * (2 * side),
        compiler_params=pltpu.CompilerParams(vmem_limit_bytes=16 * MIB),
        cost_estimate=pl.CostEstimate(
            flops=2 * slots * tok_rows * blk * blk, bytes_accessed=8 * MIB, transcendentals=0
        ),
    )(listed, at, gathered, pg)

    def y_perm(d):
        return [(side * a + b, side * a + (b + d) % side) for a in range(side) for b in range(side)]

    def x_perm(d):
        return [(side * a + b, side * ((a + d) % side) + b) for a in range(side) for b in range(side)]

    def two_hops(parts, first, then):
        got = [parts[0]] + [lax.ppermute(parts[d], "dp", first(d)) for d in range(1, side)]
        half = []
        for d in range(side):
            total = got[0][d].astype(jnp.float32)
            for g in got[1:]:
                total = total + g[d].astype(jnp.float32)
            half.append(total)
        total = half[0]
        for d in range(1, side):
            total = total + lax.ppermute(half[d].astype(bf16), "dp", then(d)).astype(jnp.float32)
        return total

    scale = 1.0 / jnp.sqrt(jnp.float32(tok_rows * n_dp))
    top = two_hops(terms[:side], y_perm, x_perm)
    bottom = two_hops(terms[side:], x_perm, y_perm)
    own_grads = jnp.concatenate([top, bottom], axis=1) * scale
    return act, in_grad, own_grads[None]


def solution(mesh):
    return jax.shard_map(
        functools.partial(on_device, mesh.shape["dp"], mesh.shape["blk"]),
        mesh=mesh,
        in_specs=(
            P("dp", "blk"),
            P("blk", None, None, None),
            P("blk", None, None),
            P(),
            P("dp", "blk"),
        ),
        out_specs=(P("dp", "blk"), P("dp", "blk"), P("blk", "dp", None, None)),
        check_vma=False,
    )
```

```python
import functools

import jax
import jax.numpy as jnp
import numpy as np
from jax import lax
from jax.experimental import pallas as pl
from jax.experimental.pallas import tpu as pltpu
from jax.sharding import PartitionSpec as P

SMEM = pl.BlockSpec(memory_space=pltpu.SMEM)
VMEM = pl.BlockSpec(memory_space=pltpu.VMEM)
MIB = 1 << 20
BF16, F32 = jnp.bfloat16, jnp.float32
NZ = 16

UP_OWN = {0: 0, 4: 2, 2: 4, 6: 6, 1: 9, 5: 11, 3: 13, 7: 15}
UP_OTHER = {4: 17, 2: 19, 6: 21, 1: 24, 5: 26, 3: 28, 7: 30}
DOWN = {1: 0, 5: 2, 3: 4, 7: 6, 4: 9, 2: 11, 6: 13}


def place_tables():
    up, down = np.zeros(2 * NZ, np.int32), np.zeros(2 * NZ, np.int32)
    for i in range(NZ):
        for e in range(2):
            if i < 8:
                up[2 * i + e] = UP_OWN[i] + e
            elif i == 8:
                up[2 * i + e] = (8, 23)[e]
            else:
                up[2 * i + e] = UP_OTHER[NZ - i] + 1 - e
            if i == 0:
                down[2 * i + e] = 8 + 16 * e
            elif i < 8:
                down[2 * i + e] = DOWN[i] + e
            elif i == 8:
                down[2 * i + e] = 15 + 16 * e
            else:
                down[2 * i + e] = 16 + DOWN[NZ - i] + 1 - e
    return up, down


def params(mib):
    return pltpu.CompilerParams(vmem_limit_bytes=mib * MIB)


def cost(flops, size):
    return pl.CostEstimate(flops=flops, bytes_accessed=size, transcendentals=0)


def shape(*dims, dtype=BF16):
    return jax.ShapeDtypeStruct(dims, dtype)


def key_of(dev, me):
    step = lax.rem(dev // 2 - me[0] + NZ, NZ)
    step = jnp.where(me[1] == 0, step, lax.rem(NZ - step, NZ))
    return 2 * step + (dev % 2 != me[1]).astype(jnp.int32)


def at(i, size):
    return pl.ds(pl.multiple_of(i * size, size), size)


def lay_weights(rows_per_dev, listed, cut, me, up_at, down_at, w_ref, up_ref, own_ref, other_ref, place):
    slots, blk = w_ref.shape[0], w_ref.shape[1]

    def note(p, carry):
        place[cut[p]] = p
        return carry

    lax.fori_loop(0, cut.shape[0], note, 0)
    for ref in (up_ref, own_ref, other_ref):
        ref[...] = jnp.zeros_like(ref)

    def put(s, carry):
        row, col = listed[2 * s], listed[2 * s + 1]

        @pl.when(row >= 0)
        def _():
            block = w_ref[s]
            up = up_at[key_of(row // rows_per_dev, me)]
            up_ref[at(up * rows_per_dev + row % rows_per_dev, blk), at(col, blk)] = block
            to = place[row]
            down = down_at[key_of(to // rows_per_dev, me)]
            a = to % rows_per_dev
            flipped = block.T

            @pl.when(down < 16)
            def _():
                own_ref[down, at(col, blk), at(a, blk)] = flipped

            @pl.when(down >= 16)
            def _():
                other_ref[down - 16, at(col, blk), at(a, blk)] = flipped

        return carry

    lax.fori_loop(0, slots, put, 0)


def times(up_ref, first, *x_refs):
    parts = []
    for ref in x_refs:
        parts += [ref[n] for n in range(ref.shape[0])] if len(ref.shape) == 3 else [ref[...]]
    x = jnp.concatenate(parts, axis=1)
    feats = parts[0].shape[1]
    return jnp.dot(x, up_ref[first * feats : (first + len(parts)) * feats], preferred_element_type=F32)


def forward_early(a_ref, g8_ref, up_ref, out_ref):
    out_ref[...] = times(up_ref, 0, a_ref, g8_ref)


def forward_late(so_far, l_ref, b_ref, up_ref, out_ref):
    out_ref[...] = so_far[...] + times(up_ref, 9, l_ref, b_ref)


def forward_last(so_far, s_ref, up_ref, og_ref, act_ref, pg_ref):
    hidden = so_far[...] + times(up_ref, 24, s_ref)
    sig = jax.nn.sigmoid(hidden)
    act_ref[...] = (hidden * sig).astype(BF16)
    pg_ref[...] = (og_ref[...].astype(F32) * sig * (1.0 + hidden * (1.0 - sig))).astype(BF16)


def back(first, pg_ref, pg2_ref, own_ref, sibling_ref, out_ref):
    for n in range(out_ref.shape[0]):
        out_ref[n] = (
            jnp.dot(pg_ref[...], own_ref[first + n], preferred_element_type=F32)
            + jnp.dot(pg2_ref[...], sibling_ref[first + n], preferred_element_type=F32)
        ).astype(out_ref.dtype)


def back_away(pg_ref, pg2_ref, own_ref, sibling_ref, out_ref, last_ref):
    back(0, pg_ref, pg2_ref, own_ref, sibling_ref, out_ref)
    last_ref[...] = (
        jnp.dot(pg_ref[...], own_ref[15], preferred_element_type=F32)
        + jnp.dot(pg2_ref[...], sibling_ref[15], preferred_element_type=F32)
    ).astype(BF16)


def f32(v):
    return v.astype(F32)


def add_first(d_ref, r1_ref, out_ref):
    for n in range(4):
        out_ref[n] = (d_ref[3 + n] + f32(r1_ref[4 + n])).astype(BF16)


def add_second(d_ref, r1_ref, r2_ref, r8_ref, out_ref):
    out_ref[0] = (d_ref[1] + f32(r1_ref[2]) + f32(r2_ref[2]) + f32(r8_ref[...])).astype(BF16)
    out_ref[1] = (d_ref[2] + f32(r1_ref[3]) + f32(r2_ref[3])).astype(BF16)


def add_third(r1_ref, r2_ref, r3_ref, out_ref):
    out_ref[...] = (f32(r1_ref[1]) + f32(r2_ref[1]) + f32(r3_ref[1])).astype(BF16)


def add_last(d_ref, r1_ref, r2_ref, r3_ref, r4_ref, out_ref):
    total = d_ref[0] + f32(r1_ref[0]) + f32(r2_ref[0]) + f32(r3_ref[0]) + f32(r4_ref[...])
    out_ref[...] = total.astype(BF16)


def weight_terms(rows_per_dev, listed, me, up_at, pg_ref, a_ref, g8_ref, l_ref, b_ref, s_ref, out_ref, flipped):
    slots, blk = out_ref.shape[0], out_ref.shape[1]
    flipped[...] = pg_ref[...].T

    def one(s, carry):
        row, col = listed[2 * s], listed[2 * s + 1]
        up = up_at[key_of(jnp.maximum(row, 0) // rows_per_dev, me)]
        lanes = at(jnp.maximum(row, 0) % rows_per_dev, blk)

        def term(x):
            out_ref[s] = jnp.dot(flipped[at(col, blk), :], x, preferred_element_type=F32).astype(BF16)

        def when(low, high):
            return pl.when((row >= 0) & (up >= low) & (up < high))

        @when(0, 8)
        def _():
            term(a_ref[up, :, lanes])

        @when(8, 9)
        def _():
            term(g8_ref[:, lanes])

        @when(9, 17)
        def _():
            term(l_ref[up - 9, :, lanes])

        @when(17, 24)
        def _():
            term(b_ref[up - 17, :, lanes])

        @when(24, 32)
        def _():
            term(s_ref[up - 24, :, lanes])

        @pl.when(row < 0)
        def _():
            out_ref[s] = jnp.zeros((blk, blk), BF16)

        return carry

    lax.fori_loop(0, slots, one, 0)


def add_terms(scale, in_ref, out_ref):
    for q in range(out_ref.shape[0]):
        total = f32(in_ref[0, q])
        for g in range(1, in_ref.shape[0]):
            total = total + f32(in_ref[g, q])
        out_ref[q] = total.T * scale


def kernel(body, out, smem=0, n_in=1, mib=16, flops=0, size=MIB, scratch=()):
    several = isinstance(out, tuple)
    return pl.pallas_call(
        body,
        out_shape=out,
        in_specs=[SMEM] * smem + [VMEM] * n_in,
        out_specs=(VMEM,) * len(out) if several else VMEM,
        scratch_shapes=scratch,
        compiler_params=params(mib),
        cost_estimate=cost(flops, size),
    )


def on_device(n_dp, tokens, up_blocks, block_list, row_cut, out_grad):
    tok_rows, feats = tokens.shape
    slots, blk = up_blocks.shape[1], up_blocks.shape[2]
    width = out_grad.shape[1]
    rows_per_dev = row_cut.shape[1]
    per = slots // n_dp
    listed = block_list.reshape(-1)
    cut = row_cut.reshape(-1)
    blk_at = lax.axis_index("blk")
    me = jnp.stack([blk_at // 2, blk_at % 2]).astype(jnp.int32)
    up_np, down_np = place_tables()
    up_at, down_at = jnp.asarray(up_np), jnp.asarray(down_np)
    shard = 2 * tok_rows * feats

    def other_core(v):
        return lax.ppermute(v, "blk", [(n, n ^ 1) for n in range(2 * NZ)])

    def steps(v, d):
        pairs = [(2 * z + c, 2 * ((z + (d, -d)[c]) % NZ) + c) for z in range(NZ) for c in range(2)]
        return lax.ppermute(v, "blk", pairs)

    def flops_of(shards):
        return 2 * shards * tok_rows * feats * width

    together = lax.optimization_barrier
    theirs = other_core(tokens)
    theirs, listed, cut = together((theirs, listed, cut))
    g0 = jnp.stack([tokens, theirs])
    g4 = steps(g0, -4)

    up_w, down_w, down_other = kernel(
        functools.partial(lay_weights, rows_per_dev),
        (shape(2 * NZ * feats, width),) + (shape(NZ, width, feats),) * 2,
        smem=5, mib=24, size=20 * MIB, scratch=[pltpu.SMEM((cut.shape[0],), jnp.int32)],
    )(listed, cut, me, up_at, down_at, up_blocks[0])
    g4, up_w, down_other = together((g4, up_w, down_other))
    down_sibling = other_core(down_other)

    g26 = steps(jnp.concatenate([g0, g4]), -2)
    g8 = steps(g4[0], -4)
    g26, g8 = together((g26, g8))
    early = jnp.concatenate([g0, g4, g26])
    late = steps(early, -1)
    early_other = other_core(jnp.concatenate([g4, g26, g8[None]]))

    hidden_shape = shape(tok_rows, width, dtype=F32)
    hidden = kernel(forward_early, hidden_shape, n_in=3, flops=flops_of(9), size=4 * MIB)(early, g8, up_w)
    late, hidden, early_other = together((late, hidden, early_other))
    late_other = other_core(late)
    hidden = kernel(forward_late, hidden_shape, n_in=4, flops=flops_of(15), size=6 * MIB)(
        hidden, late, early_other, up_w
    )
    act, pg = kernel(forward_last, (shape(tok_rows, width),) * 2, n_in=4, flops=flops_of(8), size=4 * MIB)(
        hidden, late_other, up_w, out_grad
    )
    pg2 = other_core(pg)

    d1, d8 = kernel(back_away, (shape(8, tok_rows, feats), shape(tok_rows, feats)), n_in=4, flops=flops_of(18), size=6 * MIB)(
        pg, pg2, down_w, down_sibling
    )
    r1 = steps(d1, 1)
    r8 = steps(d8, 4)
    d2 = kernel(functools.partial(back, 8), shape(7, tok_rows, feats, dtype=F32), n_in=4, flops=flops_of(14), size=6 * MIB)(
        pg, pg2, down_w, down_sibling
    )
    pg_after, d2 = together((pg, d2))
    terms = kernel(
        functools.partial(weight_terms, rows_per_dev), shape(slots, blk, blk), smem=3, n_in=6,
        flops=2 * slots * tok_rows * blk * blk, size=8 * MIB, scratch=[pltpu.VMEM((width, tok_rows), BF16)],
    )(listed, me, up_at, pg_after, early, g8, late, early_other, late_other)
    r1, r8, terms = together((r1, r8, terms))
    got = lax.all_to_all(terms, "dp", 0, 0, tiled=True)

    q26 = kernel(add_first, shape(4, tok_rows, feats), n_in=2)(d2, r1)
    r2 = steps(q26, 2)
    q4 = kernel(add_second, shape(2, tok_rows, feats), n_in=4)(d2, r1, r2, r8)
    r3 = steps(q4, 4)
    q0 = kernel(add_third, shape(tok_rows, feats), n_in=3)(r1, r2, r3)
    r4 = other_core(q0)
    in_grad = kernel(add_last, shape(tok_rows, feats), n_in=5)(d2, r1, r2, r3, r4)

    own_grads = kernel(
        functools.partial(add_terms, 1.0 / (tok_rows * n_dp) ** 0.5), shape(per, blk, blk, dtype=F32), size=3 * MIB
    )(got.reshape(n_dp, per, blk, blk))
    return act, in_grad, own_grads[None]


def solution(mesh):
    return jax.shard_map(
        functools.partial(on_device, mesh.shape["dp"]),
        mesh=mesh,
        in_specs=(
            P("dp", "blk"),
            P("blk", None, None, None),
            P("blk", None, None),
            P(),
            P("dp", "blk"),
        ),
        out_specs=(P("dp", "blk"), P("dp", "blk"), P("blk", "dp", None, None)),
        check_vma=False,
    )
```

```python
import functools

import jax
import jax.numpy as jnp
from jax import lax
from jax.experimental import pallas as pl
from jax.experimental.pallas import tpu as pltpu
from jax.sharding import PartitionSpec as P

SMEM = pl.BlockSpec(memory_space=pltpu.SMEM)
VMEM = pl.BlockSpec(memory_space=pltpu.VMEM)
HBM = pl.BlockSpec(memory_space=pltpu.HBM)
MIB = 1 << 20
BF16, F32 = jnp.bfloat16, jnp.float32
NZ = 16


def params(mib):
    return pltpu.CompilerParams(vmem_limit_bytes=mib * MIB)


def cost(flops, size):
    return pl.CostEstimate(flops=flops, bytes_accessed=size, transcendentals=0)


def shape(*dims, dtype=BF16):
    return jax.ShapeDtypeStruct(dims, dtype)


def my_place():
    here = lax.axis_index("blk")
    return here // 2, lax.rem(here, 2)


def place_of(dev, me):
    z, core = me
    step = lax.rem(dev // 2 - z + NZ, NZ)
    chosen = (step >= NZ // 2).astype(jnp.int32)
    i = jnp.where(step < NZ // 2, step, NZ - 1 - step)
    order = 4 * lax.rem(i, 2) + i // 4 + 2 * lax.rem(i // 2, 2)
    return chosen == core, 2 * order + (lax.rem(dev, 2) != chosen).astype(jnp.int32)


def in_hbm(v):
    return pltpu.with_memory_space_constraint(v, pltpu.HBM)


def at(i, size):
    return pl.ds(pl.multiple_of(i * size, size), size)


def lay_weights(listed_hbm, cut_hbm, w_hbm, up_ref, own_ref, other_ref, listed, cut, place, w_ref, sems):
    copies = [
        pltpu.make_async_copy(src, dst, sems.at[n])
        for n, (src, dst) in enumerate(((listed_hbm, listed), (cut_hbm, cut), (w_hbm, w_ref)))
    ]
    for copy in copies:
        copy.start()
    slots, blk = w_ref.shape[0], w_ref.shape[1]
    rows_per_dev, devs = cut.shape
    me = my_place()

    def note(k, carry):
        for a in range(rows_per_dev):
            place[cut[a, k]] = k * rows_per_dev + a
        return carry

    for ref in (up_ref, own_ref, other_ref):
        ref[...] = jnp.zeros_like(ref)
    for copy in copies:
        copy.wait()
    lax.fori_loop(0, devs, note, 0)

    def put(s, carry):
        row, col = listed[0, s], listed[1, s]

        @pl.when(row >= 0)
        def _():
            block = w_ref[s]
            mine, n = place_of(row // rows_per_dev, me)
            n = jnp.where(mine, n, n + NZ)
            up_ref[at(n * rows_per_dev + lax.rem(row, rows_per_dev), blk), at(col, blk)] = block
            to = place[row]
            mine, n = place_of(to // rows_per_dev, me)
            a = lax.rem(to, rows_per_dev)
            flipped = block.T

            @pl.when(mine)
            def _():
                own_ref[n, at(col, blk), at(a, blk)] = flipped

            @pl.when(jnp.logical_not(mine))
            def _():
                other_ref[n, at(col, blk), at(a, blk)] = flipped

        return carry

    lax.fori_loop(0, slots, put, 0)


def join_first(t_ref, x_ref, y_ref, out_ref):
    core = my_place()[1]

    @pl.when(core == 0)
    def _():
        out_ref[0] = t_ref[...]

    @pl.when(core != 0)
    def _():
        out_ref[0] = y_ref[...]

    out_ref[1] = x_ref[...]


def join(a_ref, b_ref, out_ref):
    n = a_ref.shape[0]
    out_ref[:n] = a_ref[...]
    out_ref[n:] = b_ref[...]


def times(up_ref, first, *x_refs):
    parts = []
    for ref in x_refs:
        parts += [ref[n] for n in range(ref.shape[0])] if len(ref.shape) == 3 else [ref[...]]
    x = jnp.concatenate(parts, axis=1)
    feats = parts[0].shape[1]
    return jnp.dot(x, up_ref[first * feats : (first + len(parts)) * feats], preferred_element_type=F32)


def forward_early(a_ref, up_ref, out_ref):
    out_ref[...] = times(up_ref, 0, a_ref)


def forward_late(so_far, l_ref, b_ref, up_ref, out_ref):
    out_ref[...] = so_far[...] + times(up_ref, 8, l_ref, b_ref)


def forward_last(so_far, s_ref, up_ref, og_ref, act_ref, pg_ref):
    hidden = so_far[...] + times(up_ref, 24, s_ref)
    sig = jax.nn.sigmoid(hidden)
    act_ref[...] = (hidden * sig).astype(BF16)
    pg_ref[...] = (og_ref[...].astype(F32) * sig * (1.0 + hidden * (1.0 - sig))).astype(BF16)


def back(first, pg_ref, pg2_ref, own_ref, sibling_ref, out_ref):
    for n in range(out_ref.shape[0]):
        out_ref[n] = (
            jnp.dot(pg_ref[...], own_ref[first + n], preferred_element_type=F32)
            + jnp.dot(pg2_ref[...], sibling_ref[first + n], preferred_element_type=F32)
        ).astype(out_ref.dtype)


def f32(v):
    return v.astype(F32)


def add_first(d_ref, r1_ref, out_ref):
    for n in range(4):
        out_ref[n] = (d_ref[4 + n] + f32(r1_ref[4 + n])).astype(BF16)


def add_second(d_ref, r1_ref, r2_ref, out_ref):
    for n in range(2):
        out_ref[n] = (d_ref[2 + n] + f32(r1_ref[2 + n]) + f32(r2_ref[2 + n])).astype(BF16)


def add_third(d_ref, r1_ref, r2_ref, r3_ref, same_ref, cross_ref):
    for n, out_ref in enumerate((same_ref, cross_ref)):
        out_ref[...] = (d_ref[n] + f32(r1_ref[n]) + f32(r2_ref[n]) + f32(r3_ref[n])).astype(BF16)


def add_last(same_ref, cross_ref, moved_ref, out_ref):
    core = my_place()[1]

    @pl.when(core == 0)
    def _():
        out_ref[...] = (f32(same_ref[...]) + f32(cross_ref[...])).astype(BF16)

    @pl.when(core != 0)
    def _():
        out_ref[...] = (f32(moved_ref[...]) + f32(cross_ref[...])).astype(BF16)


def weight_terms(listed_hbm, pg_ref, a_ref, l_ref, b_ref, s_ref, out_ref, listed, flipped, dense, sem):
    fetch = pltpu.make_async_copy(listed_hbm, listed, sem)
    fetch.start()
    slots, blk = out_ref.shape[0], out_ref.shape[1]
    rows_per_dev = dense.shape[2] // blk
    me = my_place()
    flipped[...] = pg_ref[...].T
    for m, ref in enumerate((a_ref, l_ref, b_ref, s_ref)):
        for n in range(ref.shape[0]):
            dense[8 * m + n] = jnp.dot(flipped[...], ref[n], preferred_element_type=F32).astype(BF16)

    fetch.wait()

    def one(s, carry):
        row, col = listed[0, s], listed[1, s]
        used = row >= 0
        row, col = jnp.maximum(row, 0), jnp.maximum(col, 0)
        mine, n = place_of(row // rows_per_dev, me)
        n = jnp.where(mine, n, n + NZ)
        block = dense[n, at(col, blk), at(lax.rem(row, rows_per_dev), blk)]
        out_ref[s] = jnp.where(used, block, jnp.zeros_like(block))
        return carry

    lax.fori_loop(0, slots, one, 0, unroll=4)


def add_terms(scale, in_ref, out_ref):
    for q in range(out_ref.shape[0]):
        total = f32(in_ref[0, q])
        for g in range(1, in_ref.shape[0]):
            total = total + f32(in_ref[g, q])
        out_ref[q] = total.T * scale


def kernel(body, out, ins=(), n_in=1, mib=16, flops=0, size=MIB, scratch=()):
    several = isinstance(out, tuple)
    return pl.pallas_call(
        body,
        out_shape=out,
        in_specs=list(ins) + [VMEM] * n_in,
        out_specs=(VMEM,) * len(out) if several else VMEM,
        scratch_shapes=scratch,
        compiler_params=params(mib),
        cost_estimate=cost(flops, size),
    )


def on_device(n_dp, tokens, up_blocks, block_list, row_cut, out_grad):
    tok_rows, feats = tokens.shape
    slots, blk = up_blocks.shape[1], up_blocks.shape[2]
    width = out_grad.shape[1]
    rows_per_dev = row_cut.shape[1]
    per = slots // n_dp
    listed, cut = block_list[0].T, row_cut.T
    around = range(NZ)
    together = lax.optimization_barrier

    def send(v, pairs):
        return lax.ppermute(v, "blk", pairs)

    def other_core(v):
        return send(v, [(n, n ^ 1) for n in range(2 * NZ)])

    def steps(v, d):
        return send(v, [(2 * z + c, 2 * ((z + (d, -d)[c]) % NZ) + c) for z in around for c in range(2)])

    def flops_of(shards):
        return 2 * shards * tok_rows * feats * width

    def shards(n, dtype=BF16):
        return shape(n, tok_rows, feats, dtype=dtype)

    cross_pairs = [(2 * z + 1, 2 * z) for z in around] + [(2 * z, 2 * ((z + 1) % NZ) + 1) for z in around]
    along_pairs = [(2 * z + 1, 2 * ((z + 1) % NZ) + 1) for z in around]

    crossed, along = send(tokens, cross_pairs), send(tokens, along_pairs)
    g0 = kernel(join_first, shards(2), n_in=3)(tokens, crossed, along)
    g0, listed = together((g0, listed))
    g4 = steps(g0, -4)
    up_w, down_w, down_other = kernel(
        lay_weights,
        (shape(2 * NZ * feats, width),) + (shape(NZ, width, feats),) * 2,
        ins=[HBM] * 3, n_in=0, mib=24, size=20 * MIB,
        scratch=[
            pltpu.SMEM(listed.shape, jnp.int32), pltpu.SMEM(cut.shape, jnp.int32), pltpu.SMEM((cut.size,), jnp.int32),
            pltpu.VMEM((slots, blk, blk), BF16), pltpu.SemaphoreType.DMA((3,)),
        ],
    )(in_hbm(listed), in_hbm(cut), in_hbm(up_blocks[0]))
    g4, up_w, down_other = together((g4, up_w, down_other))
    down_sibling = other_core(down_other)

    g04 = kernel(join, shards(4), n_in=2)(g0, g4)
    early = kernel(join, shards(8), n_in=2)(g04, steps(g04, -2))
    late = steps(early, -1)
    hidden_shape = shape(tok_rows, width, dtype=F32)
    hidden = kernel(forward_early, hidden_shape, n_in=2, flops=flops_of(8), size=4 * MIB)(early, up_w)
    early_other = other_core(early)
    late, hidden, early_other = together((late, hidden, early_other))
    late_other = other_core(late)
    hidden = kernel(forward_late, hidden_shape, n_in=4, flops=flops_of(16), size=6 * MIB)(
        hidden, late, early_other, up_w
    )
    act, pg = kernel(forward_last, (shape(tok_rows, width),) * 2, n_in=4, flops=flops_of(8), size=4 * MIB)(
        hidden, late_other, up_w, out_grad
    )
    pg2 = other_core(pg)

    d1 = kernel(functools.partial(back, 8), shards(8), n_in=4, flops=flops_of(16), size=6 * MIB)(
        pg, pg2, down_w, down_sibling
    )
    pg_after, d1 = together((pg, d1))
    r1 = steps(d1, 1)
    d2 = kernel(functools.partial(back, 0), shards(8, F32), n_in=4, flops=flops_of(16), size=6 * MIB)(
        pg, pg2, down_w, down_sibling
    )
    pg_after, d2 = together((pg_after, d2))
    terms = kernel(
        weight_terms, shape(slots, blk, blk), ins=[HBM], n_in=5, mib=14,
        flops=flops_of(32), size=16 * MIB,
        scratch=[
            pltpu.SMEM(listed.shape, jnp.int32), pltpu.VMEM((width, tok_rows), BF16),
            pltpu.VMEM((2 * NZ, width, feats), BF16), pltpu.SemaphoreType.DMA,
        ],
    )(in_hbm(listed), pg_after, early, late, early_other, late_other)
    r1, terms = together((r1, terms))
    got = lax.all_to_all(terms, "dp", 0, 0, tiled=True)
    q26 = kernel(add_first, shards(4), n_in=2)(d2, r1)
    r2 = steps(q26, 2)
    q4 = kernel(add_second, shards(2), n_in=3, flops=10**11)(d2, r1, r2)
    r3 = steps(q4, 4)
    one = shape(tok_rows, feats)
    same, cross = kernel(add_third, (one, one), n_in=4)(d2, r1, r2, r3)
    crossed = send(cross, [(b, a) for a, b in cross_pairs])
    moved = send(same, [(b, a) for a, b in along_pairs])
    in_grad = kernel(add_last, one, n_in=3)(same, crossed, moved)

    own_grads = kernel(
        functools.partial(add_terms, 1.0 / (tok_rows * n_dp) ** 0.5), shape(per, blk, blk, dtype=F32), size=3 * MIB
    )(got.reshape(n_dp, per, blk, blk))
    return act, in_grad, own_grads[None]


def solution(mesh):
    return jax.shard_map(
        functools.partial(on_device, mesh.shape["dp"]),
        mesh=mesh,
        in_specs=(
            P("dp", "blk"),
            P("blk", None, None, None),
            P("blk", None, None),
            P(),
            P("dp", "blk"),
        ),
        out_specs=(P("dp", "blk"), P("dp", "blk"), P("blk", "dp", None, None)),
        check_vma=False,
    )
```

```python
import functools

import jax
import jax.numpy as jnp
from jax import lax
from jax.experimental import pallas as pl
from jax.experimental.pallas import tpu as pltpu
from jax.sharding import PartitionSpec as P

SMEM = pl.BlockSpec(memory_space=pltpu.SMEM)
VMEM = pl.BlockSpec(memory_space=pltpu.VMEM)
HBM = pl.BlockSpec(memory_space=pltpu.HBM)
MIB = 1 << 20
BF16, F32 = jnp.bfloat16, jnp.float32
NZ = 16
JOIN = 80 * 10**9


def params(mib):
    return pltpu.CompilerParams(vmem_limit_bytes=mib * MIB)


def cost(flops, size):
    return pl.CostEstimate(flops=flops, bytes_accessed=size, transcendentals=0)


def shape(*dims, dtype=BF16):
    return jax.ShapeDtypeStruct(dims, dtype)


def my_place():
    here = lax.axis_index("blk")
    return here // 2, lax.rem(here, 2)


def place_of(dev, me):
    z, core = me
    step = lax.rem(dev // 2 - z + NZ, NZ)
    chosen = (step >= NZ // 2).astype(jnp.int32)
    i = jnp.where(step < NZ // 2, step, NZ - 1 - step)
    stream = (lax.rem(dev, 2) != chosen).astype(jnp.int32)
    return chosen == core, 8 * lax.rem(i, 2) + 4 * stream + i // 4 + 2 * lax.rem(i // 2, 2)


def in_hbm(v):
    return pltpu.with_memory_space_constraint(v, pltpu.HBM)


def at(i, size):
    return pl.ds(pl.multiple_of(i * size, size), size)


def lay_weights(listed_hbm, cut_hbm, w_hbm, up_ref, own_ref, other_ref, listed, cut, place, w_ref, sems):
    copies = [
        pltpu.make_async_copy(src, dst, sems.at[n])
        for n, (src, dst) in enumerate(((listed_hbm, listed), (cut_hbm, cut), (w_hbm, w_ref)))
    ]
    for copy in copies:
        copy.start()
    slots, blk = w_ref.shape[0], w_ref.shape[1]
    rows_per_dev, devs = cut.shape
    me = my_place()

    def note(k, carry):
        for a in range(rows_per_dev):
            place[cut[a, k]] = k * rows_per_dev + a
        return carry

    for ref in (up_ref, own_ref, other_ref):
        ref[...] = jnp.zeros_like(ref)
    for copy in copies:
        copy.wait()
    lax.fori_loop(0, devs, note, 0)

    def put(s, carry):
        row, col = listed[0, s], listed[1, s]

        @pl.when(row >= 0)
        def _():
            block = w_ref[s]
            mine, n = place_of(row // rows_per_dev, me)
            n = jnp.where(mine, n, n + NZ)
            up_ref[at(n * rows_per_dev + lax.rem(row, rows_per_dev), blk), at(col, blk)] = block
            to = place[row]
            mine, n = place_of(to // rows_per_dev, me)
            a = lax.rem(to, rows_per_dev)
            flipped = block.T

            @pl.when(mine)
            def _():
                own_ref[n, at(col, blk), at(a, blk)] = flipped

            @pl.when(jnp.logical_not(mine))
            def _():
                other_ref[n, at(col, blk), at(a, blk)] = flipped

        return carry

    lax.fori_loop(0, slots, put, 0)


def pair_up(a_ref, b_ref, out_ref):
    out_ref[0] = a_ref[...]
    out_ref[1] = b_ref[...]


def chosen_base(core_0_ref, core_1_ref, use):
    core = my_place()[1]

    @pl.when(core == 0)
    def _():
        use(core_0_ref)

    @pl.when(core != 0)
    def _():
        use(core_1_ref)


def join_base(stream, pair_ref, hop_ref, g4_ref, out_ref):
    def put(ref):
        out_ref[0] = ref[stream]

    chosen_base(pair_ref, hop_ref, put)
    out_ref[1] = g4_ref[...]


def join(a_ref, b_ref, out_ref):
    n = a_ref.shape[0]
    out_ref[:n] = a_ref[...]
    out_ref[n:] = b_ref[...]


def times(up_ref, first, *x_refs):
    parts = []
    for ref in x_refs:
        parts += [ref[n] for n in range(ref.shape[0])] if len(ref.shape) == 3 else [ref[...]]
    x = jnp.concatenate(parts, axis=1)
    feats = parts[0].shape[1]
    return jnp.dot(x, up_ref[first * feats : (first + len(parts)) * feats], preferred_element_type=F32)


def forward_early(a_ref, b_ref, up_ref, out_ref):
    out_ref[...] = times(up_ref, 0, a_ref, b_ref)


def forward_next(so_far, la_ref, a_ref, b_ref, up_ref, out_ref):
    out_ref[...] = so_far[...] + times(up_ref, 8, la_ref) + times(up_ref, 16, a_ref, b_ref)


def forward_late(so_far, lb_ref, la_ref, up_ref, out_ref):
    out_ref[...] = so_far[...] + times(up_ref, 12, lb_ref) + times(up_ref, 24, la_ref)


def forward_last(so_far, lb_ref, up_ref, og_ref, act_ref, pg_ref):
    hidden = so_far[...] + times(up_ref, 28, lb_ref)
    sig = jax.nn.sigmoid(hidden)
    act_ref[...] = (hidden * sig).astype(BF16)
    pg_ref[...] = (og_ref[...].astype(F32) * sig * (1.0 + hidden * (1.0 - sig))).astype(BF16)


def back(first, pg_ref, pg2_ref, own_ref, sibling_ref, out_ref):
    for n in range(out_ref.shape[0]):
        out_ref[n] = (
            jnp.dot(pg_ref[...], own_ref[first + n], preferred_element_type=F32)
            + jnp.dot(pg2_ref[...], sibling_ref[first + n], preferred_element_type=F32)
        ).astype(out_ref.dtype)


def f32(v):
    return v.astype(F32)


def add_first(d_ref, r1_ref, out_ref):
    for n in range(2):
        out_ref[n] = (d_ref[2 + n] + f32(r1_ref[2 + n])).astype(BF16)


def add_second(d_ref, r1_ref, r2_ref, out_ref):
    out_ref[...] = (d_ref[1] + f32(r1_ref[1]) + f32(r2_ref[1])).astype(BF16)


def add_base(da_ref, r1a_ref, r2a_ref, db_ref, r1b_ref, r2b_ref, out_ref):
    out_ref[0] = (da_ref[0] + f32(r1a_ref[0]) + f32(r2a_ref[0])).astype(BF16)
    out_ref[1] = (db_ref[0] + f32(r1b_ref[0]) + f32(r2b_ref[0])).astype(BF16)


def add_cross(base_ref, hop_ref, r3b_ref, out_ref):
    def put(ref):
        out_ref[...] = (f32(ref[1]) + f32(r3b_ref[...])).astype(BF16)

    chosen_base(base_ref, hop_ref, put)


def add_last(base_ref, hop_ref, r3a_ref, cross_ref, out_ref):
    def put(ref):
        out_ref[...] = (f32(ref[0]) + f32(r3a_ref[...]) + f32(cross_ref[...])).astype(BF16)

    chosen_base(base_ref, hop_ref, put)


def weight_terms(listed_hbm, pg_ref, *refs):
    x_refs, (out_ref, listed, flipped, dense, sem) = refs[:8], refs[8:]
    fetch = pltpu.make_async_copy(listed_hbm, listed, sem)
    fetch.start()
    slots, blk = out_ref.shape[0], out_ref.shape[1]
    rows_per_dev = dense.shape[2] // blk
    me = my_place()
    flipped[...] = pg_ref[...].T
    for m, ref in enumerate(x_refs):
        for n in range(ref.shape[0]):
            dense[4 * m + n] = jnp.dot(flipped[...], ref[n], preferred_element_type=F32).astype(BF16)

    fetch.wait()

    def one(s, carry):
        row, col = listed[0, s], listed[1, s]
        used = row >= 0
        row, col = jnp.maximum(row, 0), jnp.maximum(col, 0)
        mine, n = place_of(row // rows_per_dev, me)
        n = jnp.where(mine, n, n + NZ)
        block = dense[n, at(col, blk), at(lax.rem(row, rows_per_dev), blk)]
        out_ref[s] = jnp.where(used, block, jnp.zeros_like(block))
        return carry

    lax.fori_loop(0, slots, one, 0, unroll=4)


def add_terms(scale, in_ref, out_ref):
    for q in range(out_ref.shape[0]):
        total = f32(in_ref[0, q])
        for g in range(1, in_ref.shape[0]):
            total = total + f32(in_ref[g, q])
        out_ref[q] = total.T * scale


def kernel(body, out, ins=(), n_in=1, mib=16, flops=0, size=MIB, scratch=()):
    several = isinstance(out, tuple)
    return pl.pallas_call(
        body,
        out_shape=out,
        in_specs=list(ins) + [VMEM] * n_in,
        out_specs=(VMEM,) * len(out) if several else VMEM,
        scratch_shapes=scratch,
        compiler_params=params(mib),
        cost_estimate=cost(flops, size),
    )


def on_device(n_dp, tokens, up_blocks, block_list, row_cut, out_grad):
    tok_rows, feats = tokens.shape
    slots, blk = up_blocks.shape[1], up_blocks.shape[2]
    width = out_grad.shape[1]
    rows_per_dev = row_cut.shape[1]
    per = slots // n_dp
    listed, cut = block_list[0].T, row_cut.T
    around = range(NZ)
    together = lax.optimization_barrier

    def send(v, pairs):
        return lax.ppermute(v, "blk", pairs)

    def other_core(v):
        return send(v, [(n, n ^ 1) for n in range(2 * NZ)])

    def steps(v, d, d1=None):
        by = (d, -(d if d1 is None else d1))
        return send(v, [(2 * z + c, 2 * ((z + by[c]) % NZ) + c) for z in around for c in range(2)])

    def hop(v, d):
        return send(v, [(2 * z + 1, 2 * ((z + d) % NZ) + 1) for z in around])

    def flops_of(shards):
        return 2 * shards * tok_rows * feats * width

    def shards(n, dtype=BF16):
        return shape(n, tok_rows, feats, dtype=dtype)

    g4a = steps(tokens, -4, -5)
    theirs = other_core(tokens)
    g4b = steps(theirs, -4, -5)
    pair = kernel(pair_up, shards(2), n_in=2)(tokens, theirs)
    pair, listed = together((pair, listed))
    base = hop(pair, 1)
    up_w, down_w, down_other = kernel(
        lay_weights,
        (shape(2 * NZ * feats, width),) + (shape(NZ, width, feats),) * 2,
        ins=[HBM] * 3, n_in=0, mib=24, size=20 * MIB,
        scratch=[
            pltpu.SMEM(listed.shape, jnp.int32), pltpu.SMEM(cut.shape, jnp.int32), pltpu.SMEM((cut.size,), jnp.int32),
            pltpu.VMEM((slots, blk, blk), BF16), pltpu.SemaphoreType.DMA((3,)),
        ],
    )(in_hbm(listed), in_hbm(cut), in_hbm(up_blocks[0]))
    g4a, up_w = together((g4a, up_w))
    down_sibling = other_core(down_other)

    def based(n, g):
        return kernel(functools.partial(join_base, n), shards(2), n_in=3, flops=n * JOIN, size=0)(pair, base, g)

    g04a = based(0, g4a)
    g26a = steps(g04a, -2)
    g4b, g04a = together((g4b, g04a))
    g04b = based(1, g4b)
    g26b = steps(g04b, -2)
    g26a, g04b = together((g26a, g04b))
    ea = kernel(join, shards(4), n_in=2, size=0)(g04a, g26a)
    la = steps(ea, -1)
    g26b, ea, down_sibling = together((g26b, ea, down_sibling))
    eb = kernel(join, shards(4), n_in=2, flops=JOIN, size=0)(g04b, g26b)
    lb = steps(eb, -1)
    la, ea, eb = together((la, ea, eb))
    ea2, eb2 = other_core(ea), other_core(eb)

    hidden_shape = shape(tok_rows, width, dtype=F32)

    def more(body, *operands):
        return kernel(body, hidden_shape, n_in=len(operands), size=0)(*operands)

    hidden = more(forward_early, ea, eb, up_w)
    la2 = other_core(la)
    hidden = more(forward_next, hidden, la, ea2, eb2, up_w)
    lb2 = other_core(lb)
    hidden = more(forward_late, hidden, lb, la2, up_w)
    act, pg = kernel(forward_last, (shape(tok_rows, width),) * 2, n_in=4, flops=flops_of(4), size=4 * MIB)(
        hidden, lb2, up_w, out_grad
    )
    pg2 = other_core(pg)

    def back_of(first, dtype):
        return kernel(functools.partial(back, first), shards(4, dtype), n_in=4, flops=flops_of(8), size=4 * MIB)(
            pg, pg2, down_w, down_sibling
        )

    d1b = back_of(12, BF16)
    r1b = steps(d1b, 1)
    pg, d1b = together((pg, d1b))
    d1a = back_of(8, BF16)
    r1a = steps(d1a, 1)
    pg, d1a = together((pg, d1a))
    d2b, d2a = back_of(4, F32), back_of(0, F32)
    pg_after, d2b, d2a = together((pg, d2b, d2a))
    terms = kernel(
        weight_terms, shape(slots, blk, blk), ins=[HBM], n_in=9, mib=14,
        flops=flops_of(32), size=16 * MIB,
        scratch=[
            pltpu.SMEM(listed.shape, jnp.int32), pltpu.VMEM((width, tok_rows), BF16),
            pltpu.VMEM((2 * NZ, width, feats), BF16), pltpu.SemaphoreType.DMA,
        ],
    )(in_hbm(listed), pg_after, ea, eb, la, lb, ea2, eb2, la2, lb2)
    r1b, terms = together((r1b, terms))

    def in_turn(body, out, turn, *operands, flops=0):
        n = len(operands)

        def ordered(*refs):
            body(*refs[:n], refs[n + 1])
            refs[n + 2][...] = refs[n][...]

        return kernel(ordered, (out, shape(8, blk, dtype=F32)), n_in=n + 1, flops=flops)(*operands, turn)

    one = shape(tok_rows, feats)
    turn = jnp.zeros((8, blk), F32)
    q, turn = in_turn(add_first, shards(2), turn, d2b, r1b)
    r2b = steps(q, 2)
    r1a, turn = together((r1a, turn))
    q, turn = in_turn(add_first, shards(2), turn, d2a, r1a)
    r2a = steps(q, 2)
    terms, turn = together((terms, turn))
    got = lax.all_to_all(terms, "dp", 0, 0, tiled=True)
    r2b, turn = together((r2b, turn))
    q, turn = in_turn(add_second, one, turn, d2b, r1b, r2b, flops=10**11)
    r3b = steps(q, 4, 5)
    r2a, turn = together((r2a, turn))
    q, turn = in_turn(add_second, one, turn, d2a, r1a, r2a)
    r3a = steps(q, 4, 5)
    sums = kernel(add_base, shards(2), n_in=6, size=0)(d2a, r1a, r2a, d2b, r1b, r2b)
    moved = hop(sums, -1)
    own_grads = kernel(
        functools.partial(add_terms, 1.0 / (tok_rows * n_dp) ** 0.5), shape(per, blk, blk, dtype=F32), size=3 * MIB
    )(got.reshape(n_dp, per, blk, blk))
    r3b, r3a, turn = together((r3b, r3a, turn))
    q, turn = in_turn(add_cross, one, turn, sums, moved, r3b)
    cross = other_core(q)
    cross, own_grads, turn = together((cross, own_grads, turn))
    in_grad, _ = in_turn(add_last, one, turn, sums, moved, r3a, cross)
    return act, in_grad, own_grads[None]


def solution(mesh):
    return jax.shard_map(
        functools.partial(on_device, mesh.shape["dp"]),
        mesh=mesh,
        in_specs=(
            P("dp", "blk"),
            P("blk", None, None, None),
            P("blk", None, None),
            P(),
            P("dp", "blk"),
        ),
        out_specs=(P("dp", "blk"), P("dp", "blk"), P("blk", "dp", None, None)),
        check_vma=False,
    )
```

```python
import functools

import jax
import jax.numpy as jnp
from jax import lax
from jax.experimental import pallas as pl
from jax.experimental.pallas import tpu as pltpu
from jax.sharding import PartitionSpec as P

SMEM = pl.BlockSpec(memory_space=pltpu.SMEM)
VMEM = pl.BlockSpec(memory_space=pltpu.VMEM)
HBM = pl.BlockSpec(memory_space=pltpu.HBM)
MIB = 1 << 20
BF16, F32 = jnp.bfloat16, jnp.float32
NZ = 16
JOIN = 80 * 10**9
FIRST = 200 * 10**9
SECOND = 0
TURN = 10 * 10**9


def params(mib):
    return pltpu.CompilerParams(vmem_limit_bytes=mib * MIB)


def cost(flops, size):
    return pl.CostEstimate(flops=flops, bytes_accessed=size, transcendentals=0)


def shape(*dims, dtype=BF16):
    return jax.ShapeDtypeStruct(dims, dtype)


def my_place():
    here = lax.axis_index("blk")
    return here // 2, lax.rem(here, 2)


def place_of(dev, me):
    z, core = me
    step = lax.rem(dev // 2 - z + NZ, NZ)
    chosen = (step >= NZ // 2).astype(jnp.int32)
    i = jnp.where(step < NZ // 2, step, NZ - 1 - step)
    stream = (lax.rem(dev, 2) != chosen).astype(jnp.int32)
    return chosen == core, 8 * lax.rem(i, 2) + 4 * stream + i // 4 + 2 * lax.rem(i // 2, 2)


def in_hbm(v):
    return pltpu.with_memory_space_constraint(v, pltpu.HBM)


def at(i, size):
    return pl.ds(pl.multiple_of(i * size, size), size)


def lay_weights(listed_hbm, cut_hbm, w_hbm, up_ref, own_ref, other_ref, listed, cut, place, w_ref, sems):
    copies = [
        pltpu.make_async_copy(src, dst, sems.at[n])
        for n, (src, dst) in enumerate(((listed_hbm, listed), (cut_hbm, cut), (w_hbm, w_ref)))
    ]
    for copy in copies:
        copy.start()
    slots, blk = w_ref.shape[0], w_ref.shape[1]
    rows_per_dev, devs = cut.shape
    me = my_place()

    def note(k, carry):
        for a in range(rows_per_dev):
            place[cut[a, k]] = k * rows_per_dev + a
        return carry

    for ref in (up_ref, own_ref, other_ref):
        ref[...] = jnp.zeros_like(ref)
    for copy in copies:
        copy.wait()
    lax.fori_loop(0, devs, note, 0)

    def put(s, carry):
        row, col = listed[0, s], listed[1, s]

        @pl.when(row >= 0)
        def _():
            block = w_ref[s]
            mine, n = place_of(row // rows_per_dev, me)
            n = jnp.where(mine, n, n + NZ)
            up_ref[at(n * rows_per_dev + lax.rem(row, rows_per_dev), blk), at(col, blk)] = block
            to = place[row]
            mine, n = place_of(to // rows_per_dev, me)
            a = lax.rem(to, rows_per_dev)
            flipped = block.T

            @pl.when(mine)
            def _():
                own_ref[n, at(col, blk), at(a, blk)] = flipped

            @pl.when(jnp.logical_not(mine))
            def _():
                other_ref[n, at(col, blk), at(a, blk)] = flipped

        return carry

    lax.fori_loop(0, slots, put, 0)


def pair_up(a_ref, b_ref, out_ref):
    out_ref[0] = a_ref[...]
    out_ref[1] = b_ref[...]


def chosen_base(core_0_ref, core_1_ref, use):
    core = my_place()[1]

    @pl.when(core == 0)
    def _():
        use(core_0_ref)

    @pl.when(core != 0)
    def _():
        use(core_1_ref)


def join_base(stream, pair_ref, hop_ref, g4_ref, out_ref):
    def put(ref):
        out_ref[0] = ref[stream]

    chosen_base(pair_ref, hop_ref, put)
    out_ref[1] = g4_ref[...]


def join(a_ref, b_ref, out_ref):
    n = a_ref.shape[0]
    out_ref[:n] = a_ref[...]
    out_ref[n:] = b_ref[...]


def times(up_ref, first, *x_refs):
    parts = []
    for ref in x_refs:
        parts += [ref[n] for n in range(ref.shape[0])] if len(ref.shape) == 3 else [ref[...]]
    x = jnp.concatenate(parts, axis=1)
    feats = parts[0].shape[1]
    return jnp.dot(x, up_ref[first * feats : (first + len(parts)) * feats], preferred_element_type=F32)


def forward_early(a_ref, b_ref, up_ref, out_ref):
    out_ref[...] = times(up_ref, 0, a_ref, b_ref)


def forward_next(so_far, la_ref, a_ref, b_ref, up_ref, out_ref):
    out_ref[...] = so_far[...] + times(up_ref, 8, la_ref) + times(up_ref, 16, a_ref, b_ref)


def forward_late(so_far, lb_ref, la_ref, up_ref, out_ref):
    out_ref[...] = so_far[...] + times(up_ref, 12, lb_ref) + times(up_ref, 24, la_ref)


def forward_last(so_far, lb_ref, up_ref, og_ref, act_ref, pg_ref):
    hidden = so_far[...] + times(up_ref, 28, lb_ref)
    sig = jax.nn.sigmoid(hidden)
    act_ref[...] = (hidden * sig).astype(BF16)
    pg_ref[...] = (og_ref[...].astype(F32) * sig * (1.0 + hidden * (1.0 - sig))).astype(BF16)


def back(first, pg_ref, pg2_ref, own_ref, sibling_ref, out_ref):
    for n in range(out_ref.shape[0]):
        out_ref[n] = (
            jnp.dot(pg_ref[...], own_ref[first + n], preferred_element_type=F32)
            + jnp.dot(pg2_ref[...], sibling_ref[first + n], preferred_element_type=F32)
        ).astype(out_ref.dtype)


def f32(v):
    return v.astype(F32)


def add_first(d_ref, r1_ref, out_ref):
    for n in range(2):
        out_ref[n] = (d_ref[2 + n] + f32(r1_ref[2 + n])).astype(BF16)


def add_second(d_ref, r1_ref, r2_ref, next_ref, base_ref):
    for n, out_ref in enumerate((base_ref, next_ref)):
        out_ref[...] = (d_ref[n] + f32(r1_ref[n]) + f32(r2_ref[n])).astype(BF16)


def add_cross(base_ref, hop_ref, r3_ref, out_ref):
    def put(ref):
        out_ref[...] = (f32(ref[...]) + f32(r3_ref[...])).astype(out_ref.dtype)

    chosen_base(base_ref, hop_ref, put)


def add_last(own_ref, cross_ref, out_ref):
    out_ref[...] = (own_ref[...] + f32(cross_ref[...])).astype(BF16)


def weight_terms(listed_hbm, pg_ref, *refs):
    x_refs, (out_ref, listed, flipped, dense, sem) = refs[:-5], refs[-5:]
    fetch = pltpu.make_async_copy(listed_hbm, listed, sem)
    fetch.start()
    slots, blk = out_ref.shape[0], out_ref.shape[1]
    rows_per_dev = dense.shape[2] // blk
    me = my_place()
    flipped[...] = pg_ref[...].T
    for n, (ref, m) in enumerate([(ref, m) for ref in x_refs for m in range(ref.shape[0])]):
        dense[n] = jnp.dot(flipped[...], ref[m], preferred_element_type=F32).astype(BF16)

    fetch.wait()

    def one(s, carry):
        row, col = listed[0, s], listed[1, s]
        used = row >= 0
        row, col = jnp.maximum(row, 0), jnp.maximum(col, 0)
        mine, n = place_of(row // rows_per_dev, me)
        n = jnp.where(mine, n, n + NZ)
        block = dense[n, at(col, blk), at(lax.rem(row, rows_per_dev), blk)]
        out_ref[s] = jnp.where(used, block, jnp.zeros_like(block))
        return carry

    lax.fori_loop(0, slots, one, 0, unroll=4)


def add_terms(scale, in_ref, out_ref):
    for q in range(out_ref.shape[0]):
        total = f32(in_ref[0, q])
        for g in range(1, in_ref.shape[0]):
            total = total + f32(in_ref[g, q])
        out_ref[q] = total.T * scale


def kernel(body, out, ins=(), n_in=1, mib=16, flops=0, size=MIB, scratch=()):
    several = isinstance(out, tuple)
    return pl.pallas_call(
        body,
        out_shape=out,
        in_specs=list(ins) + [VMEM] * n_in,
        out_specs=(VMEM,) * len(out) if several else VMEM,
        scratch_shapes=scratch,
        compiler_params=params(mib),
        cost_estimate=cost(flops, size),
    )


def on_device(n_dp, tokens, up_blocks, block_list, row_cut, out_grad):
    tok_rows, feats = tokens.shape
    slots, blk = up_blocks.shape[1], up_blocks.shape[2]
    width = out_grad.shape[1]
    rows_per_dev = row_cut.shape[1]
    per = slots // n_dp
    listed, cut = block_list[0].T, row_cut.T
    around = range(NZ)
    together = lax.optimization_barrier

    def send(v, pairs):
        return lax.ppermute(v, "blk", pairs)

    def other_core(v):
        return send(v, [(n, n ^ 1) for n in range(2 * NZ)])

    def steps(v, d, d1=None):
        by = (d, -(d if d1 is None else d1))
        return send(v, [(2 * z + c, 2 * ((z + by[c]) % NZ) + c) for z in around for c in range(2)])

    def hop(v, d):
        return send(v, [(2 * z + 1, 2 * ((z + d) % NZ) + 1) for z in around])

    def flops_of(shards):
        return 2 * shards * tok_rows * feats * width

    def shards(n, dtype=BF16):
        return shape(n, tok_rows, feats, dtype=dtype)

    g4a = steps(tokens, -4, -5)
    theirs = other_core(tokens)
    g4b = steps(theirs, -4, -5)
    pair = kernel(pair_up, shards(2), n_in=2)(tokens, theirs)
    base = hop(pair, 1)

    def based(n, g):
        return kernel(functools.partial(join_base, n), shards(2), n_in=3, flops=n * JOIN, size=0)(pair, base, g)

    g04a = based(0, g4a)
    g26a = steps(g04a, -2)
    g4b, g04a = together((g4b, g04a))
    g04b = based(1, g4b)
    g26b = steps(g04b, -2)
    g04b, listed = together((g04b, listed))
    up_w, down_w, down_other = kernel(
        lay_weights,
        (shape(2 * NZ * feats, width),) + (shape(NZ, width, feats),) * 2,
        ins=[HBM] * 3, n_in=0, mib=24, size=20 * MIB,
        scratch=[
            pltpu.SMEM(listed.shape, jnp.int32), pltpu.SMEM(cut.shape, jnp.int32), pltpu.SMEM((cut.size,), jnp.int32),
            pltpu.VMEM((slots, blk, blk), BF16), pltpu.SemaphoreType.DMA((3,)),
        ],
    )(in_hbm(listed), in_hbm(cut), in_hbm(up_blocks[0]))
    g26a, g04b, up_w = together((g26a, g04b, up_w))
    down_sibling = other_core(down_other)
    ea = kernel(join, shards(4), n_in=2, size=0)(g04a, g26a)
    la = steps(ea, -1)
    g26b, ea = together((g26b, ea))
    eb = kernel(join, shards(4), n_in=2, flops=JOIN, size=0)(g04b, g26b)
    lb = steps(eb, -1)
    la, ea, eb = together((la, ea, eb))
    ea2, eb2 = other_core(ea), other_core(eb)

    hidden_shape = shape(tok_rows, width, dtype=F32)

    def more(body, *operands):
        return kernel(body, hidden_shape, n_in=len(operands), size=0)(*operands)

    hidden = more(forward_early, ea, eb, up_w)
    la2 = other_core(la)
    hidden = more(forward_next, hidden, la, ea2, eb2, up_w)
    lb2 = other_core(lb)
    hidden = more(forward_late, hidden, lb, la2, up_w)
    act, pg = kernel(forward_last, (shape(tok_rows, width),) * 2, n_in=4, flops=flops_of(4), size=4 * MIB)(
        hidden, lb2, up_w, out_grad
    )
    pg2 = other_core(pg)

    def back_of(first, dtype):
        return kernel(functools.partial(back, first), shards(4, dtype), n_in=4, flops=flops_of(8), size=4 * MIB)(
            pg, pg2, down_w, down_sibling
        )

    d1b = back_of(12, BF16)
    r1b = steps(d1b, 1)
    pg, d1b = together((pg, d1b))
    d1a = back_of(8, BF16)
    r1a = steps(d1a, 1)
    d2b, d2a = back_of(4, F32), back_of(0, F32)
    pg, d1a, d2b, d2a = together((pg, d1a, d2b, d2a))
    terms = kernel(
        weight_terms, shape(slots, blk, blk), ins=[HBM], n_in=9, mib=14,
        flops=flops_of(32), size=16 * MIB,
        scratch=[
            pltpu.SMEM(listed.shape, jnp.int32), pltpu.VMEM((width, tok_rows), BF16),
            pltpu.VMEM((2 * NZ, width, feats), BF16), pltpu.SemaphoreType.DMA,
        ],
    )(in_hbm(listed), pg, ea, eb, la, lb, ea2, eb2, la2, lb2)
    got = lax.all_to_all(terms, "dp", 0, 0, tiled=True)
    def in_turn(body, out, turn, *operands, flops=0):
        n = len(operands)

        def ordered(*refs):
            body(*refs[:n], *refs[n + 1 : -1])
            refs[-1][...] = refs[n][...]

        return kernel(ordered, out + (shape(8, blk, dtype=F32),), n_in=n + 1, flops=flops, size=0)(*operands, turn)

    one = shape(tok_rows, feats)
    turn = jnp.zeros((8, blk), F32)
    q, turn = in_turn(add_first, (shards(2),), turn, d2b, r1b, flops=FIRST)
    r2b = steps(q, 2)
    r1a, turn = together((r1a, turn))
    q, turn = in_turn(add_first, (shards(2),), turn, d2a, r1a, flops=SECOND)
    r2a = steps(q, 2)
    r2b, turn = together((r2b, turn))
    q, sum_b, turn = in_turn(add_second, (one, one), turn, d2b, r1b, r2b)
    r3b = steps(q, 4, 5)
    moved_b = hop(sum_b, -1)
    r2a, turn = together((r2a, turn))
    q, sum_a, turn = in_turn(add_second, (one, one), turn, d2a, r1a, r2a, flops=SECOND)
    r3a = steps(q, 4, 5)
    moved_a = hop(sum_a, -1)
    q, turn = in_turn(add_cross, (one,), turn, sum_b, moved_b, r3b)
    cross = other_core(q)
    own_grads = kernel(
        functools.partial(add_terms, 1.0 / (tok_rows * n_dp) ** 0.5), shape(per, blk, blk, dtype=F32), size=0
    )(got.reshape(n_dp, per, blk, blk))
    total = kernel(add_cross, shape(tok_rows, feats, dtype=F32), n_in=3, flops=TURN, size=0)(sum_a, moved_a, r3a)
    cross, own_grads, total, turn = together((cross, own_grads, total, turn))
    in_grad, _ = in_turn(add_last, (one,), turn, total, cross)
    return act, in_grad, own_grads[None]


def solution(mesh):
    return jax.shard_map(
        functools.partial(on_device, mesh.shape["dp"]),
        mesh=mesh,
        in_specs=(
            P("dp", "blk"),
            P("blk", None, None, None),
            P("blk", None, None),
            P(),
            P("dp", "blk"),
        ),
        out_specs=(P("dp", "blk"), P("dp", "blk"), P("blk", "dp", None, None)),
        check_vma=False,
    )
```

```python
import functools

import jax
import jax.numpy as jnp
from jax import lax
from jax.experimental import pallas as pl
from jax.experimental.pallas import tpu as pltpu
from jax.sharding import PartitionSpec as P

SMEM = pl.BlockSpec(memory_space=pltpu.SMEM)
VMEM = pl.BlockSpec(memory_space=pltpu.VMEM)
HBM = pl.BlockSpec(memory_space=pltpu.HBM)
MIB = 1 << 20
BF16, F32 = jnp.bfloat16, jnp.float32
NZ = 16
LONG = 80 * 10**9
FIRST = 200 * 10**9


def params(mib):
    return pltpu.CompilerParams(vmem_limit_bytes=mib * MIB)


def cost(flops, size):
    return pl.CostEstimate(flops=flops, bytes_accessed=size, transcendentals=0)


def shape(*dims, dtype=BF16):
    return jax.ShapeDtypeStruct(dims, dtype)


def my_place():
    here = lax.axis_index("blk")
    return here // 2, lax.rem(here, 2)


def place_of(dev, me):
    z, core = me
    step = lax.rem(dev // 2 - z + NZ, NZ)
    chosen = (step >= NZ // 2).astype(jnp.int32)
    i = jnp.where(step < NZ // 2, step, NZ - 1 - step)
    second = (lax.rem(dev, 2) != chosen).astype(jnp.int32)
    return chosen == core, 8 * lax.rem(i, 2) + 2 * (i // 4) + 4 * lax.rem(i // 2, 2) + second


def in_hbm(v):
    return pltpu.with_memory_space_constraint(v, pltpu.HBM)


def at(i, size):
    return pl.ds(pl.multiple_of(i * size, size), size)


def lay_weights(listed_hbm, cut_hbm, w_hbm, up_ref, own_ref, other_ref, listed, cut, place, w_ref, sems):
    copies = [
        pltpu.make_async_copy(src, dst, sems.at[n])
        for n, (src, dst) in enumerate(((listed_hbm, listed), (cut_hbm, cut), (w_hbm, w_ref)))
    ]
    for copy in copies:
        copy.start()
    slots, blk = w_ref.shape[0], w_ref.shape[1]
    rows_per_dev, devs = cut.shape
    me = my_place()

    def note(k, carry):
        for a in range(rows_per_dev):
            place[cut[a, k]] = k * rows_per_dev + a
        return carry

    for ref in (up_ref, own_ref, other_ref):
        ref[...] = jnp.zeros_like(ref)
    for copy in copies:
        copy.wait()
    lax.fori_loop(0, devs, note, 0)

    def put(s, carry):
        row, col = listed[0, s], listed[1, s]

        @pl.when(row >= 0)
        def _():
            block = w_ref[s]
            mine, n = place_of(row // rows_per_dev, me)
            n = jnp.where(mine, n, n + NZ)
            up_ref[at(n * rows_per_dev + lax.rem(row, rows_per_dev), blk), at(col, blk)] = block
            to = place[row]
            mine, n = place_of(to // rows_per_dev, me)
            a = lax.rem(to, rows_per_dev)
            flipped = block.T

            @pl.when(mine)
            def _():
                own_ref[n, at(col, blk), at(a, blk)] = flipped

            @pl.when(jnp.logical_not(mine))
            def _():
                other_ref[n, at(col, blk), at(a, blk)] = flipped

        return carry

    lax.fori_loop(0, slots, put, 0)


def pair_up(a_ref, b_ref, out_ref):
    out_ref[0] = a_ref[...]
    out_ref[1] = b_ref[...]


def chosen_base(core_0_ref, core_1_ref, use):
    core = my_place()[1]

    @pl.when(core == 0)
    def _():
        use(core_0_ref)

    @pl.when(core != 0)
    def _():
        use(core_1_ref)


def join_base(pair_ref, hop_ref, g4_ref, out_ref):
    def put(ref):
        out_ref[:2] = ref[...]

    chosen_base(pair_ref, hop_ref, put)
    out_ref[2:] = g4_ref[...]


def join(a_ref, b_ref, out_ref):
    n = a_ref.shape[0]
    out_ref[:n] = a_ref[...]
    out_ref[n:] = b_ref[...]


def times(up_ref, first, *x_refs):
    parts = []
    for ref in x_refs:
        parts += [ref[n] for n in range(ref.shape[0])] if len(ref.shape) == 3 else [ref[...]]
    x = jnp.concatenate(parts, axis=1)
    feats = parts[0].shape[1]
    return jnp.dot(x, up_ref[first * feats : (first + len(parts)) * feats], preferred_element_type=F32)


def forward_first(x_ref, up_ref, out_ref):
    out_ref[...] = times(up_ref, 0, x_ref)


def forward_more(place, so_far, x_ref, up_ref, out_ref):
    out_ref[...] = so_far[...] + times(up_ref, place, x_ref)


def forward_last(so_far, x_ref, up_ref, og_ref, act_ref, pg_ref):
    hidden = so_far[...] + times(up_ref, 24, x_ref)
    sig = jax.nn.sigmoid(hidden)
    act_ref[...] = (hidden * sig).astype(BF16)
    pg_ref[...] = (og_ref[...].astype(F32) * sig * (1.0 + hidden * (1.0 - sig))).astype(BF16)


def back(first, pg_ref, pg2_ref, own_ref, sibling_ref, out_ref):
    for n in range(out_ref.shape[0]):
        out_ref[n] = (
            jnp.dot(pg_ref[...], own_ref[first + n], preferred_element_type=F32)
            + jnp.dot(pg2_ref[...], sibling_ref[first + n], preferred_element_type=F32)
        ).astype(out_ref.dtype)


def f32(v):
    return v.astype(F32)


def add_first(d_ref, r1_ref, out_ref):
    for n in range(4):
        out_ref[n] = (d_ref[4 + n] + f32(r1_ref[4 + n])).astype(BF16)


def add_second(d_ref, r1_ref, r2_ref, next_ref, base_ref):
    for n in range(2):
        base_ref[n] = (d_ref[n] + f32(r1_ref[n]) + f32(r2_ref[n])).astype(BF16)
        next_ref[n] = (d_ref[2 + n] + f32(r1_ref[2 + n]) + f32(r2_ref[2 + n])).astype(BF16)


def add_third(base_ref, hop_ref, r3_ref, cross_ref, own_ref):
    def put(ref):
        cross_ref[...] = (f32(ref[1]) + f32(r3_ref[1])).astype(BF16)
        own_ref[...] = f32(ref[0]) + f32(r3_ref[0])

    chosen_base(base_ref, hop_ref, put)


def add_last(own_ref, cross_ref, out_ref):
    out_ref[...] = (own_ref[...] + f32(cross_ref[...])).astype(BF16)


def weight_terms(listed_hbm, pg_ref, *refs):
    x_refs, (out_ref, listed, flipped, dense, sem) = refs[:-5], refs[-5:]
    fetch = pltpu.make_async_copy(listed_hbm, listed, sem)
    fetch.start()
    slots, blk = out_ref.shape[0], out_ref.shape[1]
    rows_per_dev = dense.shape[2] // blk
    me = my_place()
    flipped[...] = pg_ref[...].T
    for n, (ref, m) in enumerate([(ref, m) for ref in x_refs for m in range(ref.shape[0])]):
        dense[n] = jnp.dot(flipped[...], ref[m], preferred_element_type=F32).astype(BF16)

    fetch.wait()

    def one(s, carry):
        row, col = listed[0, s], listed[1, s]
        used = row >= 0
        row, col = jnp.maximum(row, 0), jnp.maximum(col, 0)
        mine, n = place_of(row // rows_per_dev, me)
        n = jnp.where(mine, n, n + NZ)
        block = dense[n, at(col, blk), at(lax.rem(row, rows_per_dev), blk)]
        out_ref[s] = jnp.where(used, block, jnp.zeros_like(block))
        return carry

    lax.fori_loop(0, slots, one, 0, unroll=4)


def add_terms(scale, in_ref, out_ref):
    for q in range(out_ref.shape[0]):
        total = f32(in_ref[0, q])
        for g in range(1, in_ref.shape[0]):
            total = total + f32(in_ref[g, q])
        out_ref[q] = total.T * scale


def kernel(body, out, ins=(), n_in=1, mib=16, flops=0, size=MIB, scratch=()):
    several = isinstance(out, tuple)
    return pl.pallas_call(
        body,
        out_shape=out,
        in_specs=list(ins) + [VMEM] * n_in,
        out_specs=(VMEM,) * len(out) if several else VMEM,
        scratch_shapes=scratch,
        compiler_params=params(mib),
        cost_estimate=cost(flops, size),
    )


def on_device(n_dp, tokens, up_blocks, block_list, row_cut, out_grad):
    tok_rows, feats = tokens.shape
    slots, blk = up_blocks.shape[1], up_blocks.shape[2]
    width = out_grad.shape[1]
    rows_per_dev = row_cut.shape[1]
    per = slots // n_dp
    listed, cut = block_list[0].T, row_cut.T
    around = range(NZ)
    together = lax.optimization_barrier

    def send(v, pairs):
        return lax.ppermute(v, "blk", pairs)

    def other_core(v):
        return send(v, [(n, n ^ 1) for n in range(2 * NZ)])

    def steps(v, d, d1=None):
        by = (d, -(d if d1 is None else d1))
        return send(v, [(2 * z + c, 2 * ((z + by[c]) % NZ) + c) for z in around for c in range(2)])

    def hop(v, d):
        return send(v, [(2 * z + 1, 2 * ((z + d) % NZ) + 1) for z in around])

    def flops_of(shards):
        return 2 * shards * tok_rows * feats * width

    def shards(n, dtype=BF16):
        return shape(n, tok_rows, feats, dtype=dtype)

    theirs = other_core(tokens)
    pair = kernel(pair_up, shards(2), n_in=2, size=0)(tokens, theirs)
    g4 = steps(pair, -4, -5)
    base = hop(pair, 1)
    pair, listed = together((pair, listed))
    up_w, down_w, down_other = kernel(
        lay_weights,
        (shape(2 * NZ * feats, width),) + (shape(NZ, width, feats),) * 2,
        ins=[HBM] * 3, n_in=0, mib=24, size=20 * MIB,
        scratch=[
            pltpu.SMEM(listed.shape, jnp.int32), pltpu.SMEM(cut.shape, jnp.int32), pltpu.SMEM((cut.size,), jnp.int32),
            pltpu.VMEM((slots, blk, blk), BF16), pltpu.SemaphoreType.DMA((3,)),
        ],
    )(in_hbm(listed), in_hbm(cut), in_hbm(up_blocks[0]))
    g4, up_w = together((g4, up_w))
    g04 = kernel(join_base, shards(4), n_in=3, size=0)(pair, base, g4)
    g26 = steps(g04, -2)
    early = kernel(join, shards(8), n_in=2, size=0)(g04, g26)
    late = steps(early, -1)
    early, down_other = together((early, down_other))
    early_other = other_core(early)
    down_sibling = other_core(down_other)

    hidden_shape = shape(tok_rows, width, dtype=F32)

    def more(body, *operands, flops=0):
        return kernel(body, hidden_shape, n_in=len(operands), flops=flops, size=0)(*operands)

    hidden = more(forward_first, early, up_w)
    late, hidden = together((late, hidden))
    late_other = other_core(late)
    hidden = more(functools.partial(forward_more, 8), hidden, late, up_w, flops=LONG)
    hidden = more(functools.partial(forward_more, 16), hidden, early_other, up_w)
    act, pg = kernel(forward_last, (shape(tok_rows, width),) * 2, n_in=4, flops=flops_of(4), size=4 * MIB)(
        hidden, late_other, up_w, out_grad
    )
    pg2 = other_core(pg)

    def back_of(first, dtype):
        return kernel(functools.partial(back, first), shards(8, dtype), n_in=4, flops=flops_of(8), size=4 * MIB)(
            pg, pg2, down_w, down_sibling
        )

    d1 = back_of(8, BF16)
    r1 = steps(d1, 1)
    pg, d1 = together((pg, d1))
    d2 = back_of(0, F32)
    pg, d2 = together((pg, d2))
    terms = kernel(
        weight_terms, shape(slots, blk, blk), ins=[HBM], n_in=5, mib=14,
        flops=flops_of(32), size=16 * MIB,
        scratch=[
            pltpu.SMEM(listed.shape, jnp.int32), pltpu.VMEM((width, tok_rows), BF16),
            pltpu.VMEM((2 * NZ, width, feats), BF16), pltpu.SemaphoreType.DMA,
        ],
    )(in_hbm(listed), pg, early, late, early_other, late_other)
    got = lax.all_to_all(terms, "dp", 0, 0, tiled=True)

    r2 = steps(kernel(add_first, shards(4), n_in=2, flops=FIRST, size=0)(d2, r1), 2)
    q, sums = kernel(add_second, (shards(2),) * 2, n_in=3, size=0)(d2, r1, r2)
    r3 = steps(q, 4, 5)
    moved = hop(sums, -1)
    own_grads = kernel(
        functools.partial(add_terms, 1.0 / (tok_rows * n_dp) ** 0.5), shape(per, blk, blk, dtype=F32), size=0
    )(got.reshape(n_dp, per, blk, blk))
    r3, moved, own_grads = together((r3, moved, own_grads))
    one = shape(tok_rows, feats)
    cross, total = kernel(add_third, (one, shape(tok_rows, feats, dtype=F32)), n_in=3, size=0)(sums, moved, r3)
    in_grad = kernel(add_last, one, n_in=2, size=0)(total, other_core(cross))
    return act, in_grad, own_grads[None]


def solution(mesh):
    return jax.shard_map(
        functools.partial(on_device, mesh.shape["dp"]),
        mesh=mesh,
        in_specs=(
            P("dp", "blk"),
            P("blk", None, None, None),
            P("blk", None, None),
            P(),
            P("dp", "blk"),
        ),
        out_specs=(P("dp", "blk"), P("dp", "blk"), P("blk", "dp", None, None)),
        check_vma=False,
    )
```

```python
import functools

import jax
import jax.numpy as jnp
from jax import lax
from jax.experimental import pallas as pl
from jax.experimental.pallas import tpu as pltpu
from jax.sharding import PartitionSpec as P

SMEM = pl.BlockSpec(memory_space=pltpu.SMEM)
VMEM = pl.BlockSpec(memory_space=pltpu.VMEM)
HBM = pl.BlockSpec(memory_space=pltpu.HBM)
MIB = 1 << 20
BF16, F32 = jnp.bfloat16, jnp.float32
NZ = 16
LONG = 80 * 10**9
FIRST = 200 * 10**9


def params(mib):
    return pltpu.CompilerParams(vmem_limit_bytes=mib * MIB)


def cost(flops, size):
    return pl.CostEstimate(flops=flops, bytes_accessed=size, transcendentals=0)


def shape(*dims, dtype=BF16):
    return jax.ShapeDtypeStruct(dims, dtype)


def my_place():
    here = lax.axis_index("blk")
    return here // 2, lax.rem(here, 2)


def place_of(dev, me):
    z, core = me
    step = lax.rem(dev // 2 - z + NZ, NZ)
    chosen = (step >= NZ // 2).astype(jnp.int32)
    i = jnp.where(step < NZ // 2, step, NZ - 1 - step)
    second = (lax.rem(dev, 2) != chosen).astype(jnp.int32)
    return chosen == core, 8 * lax.rem(i, 2) + 2 * (i // 4) + 4 * lax.rem(i // 2, 2) + second


def in_hbm(v):
    return pltpu.with_memory_space_constraint(v, pltpu.HBM)


def at(i, size):
    return pl.ds(pl.multiple_of(i * size, size), size)


def lay_weights(listed_hbm, cut_hbm, w_hbm, up_ref, own_ref, other_ref, listed, cut, place, w_ref, sems):
    copies = [
        pltpu.make_async_copy(src, dst, sems.at[n])
        for n, (src, dst) in enumerate(((listed_hbm, listed), (cut_hbm, cut), (w_hbm, w_ref)))
    ]
    for copy in copies:
        copy.start()
    slots, blk = w_ref.shape[0], w_ref.shape[1]
    rows_per_dev, devs = cut.shape
    me = my_place()

    def note(k, carry):
        for a in range(rows_per_dev):
            place[cut[a, k]] = k * rows_per_dev + a
        return carry

    for ref in (up_ref, own_ref, other_ref):
        ref[...] = jnp.zeros_like(ref)
    for copy in copies:
        copy.wait()
    lax.fori_loop(0, devs, note, 0)

    def put(s, carry):
        row, col = listed[0, s], listed[1, s]

        @pl.when(row >= 0)
        def _():
            block = w_ref[s]
            mine, n = place_of(row // rows_per_dev, me)
            n = jnp.where(mine, n, n + NZ)
            up_ref[at(n * rows_per_dev + lax.rem(row, rows_per_dev), blk), at(col, blk)] = block
            to = place[row]
            mine, n = place_of(to // rows_per_dev, me)
            a = lax.rem(to, rows_per_dev)
            flipped = block.T

            @pl.when(mine)
            def _():
                own_ref[n, at(col, blk), at(a, blk)] = flipped

            @pl.when(jnp.logical_not(mine))
            def _():
                other_ref[n, at(col, blk), at(a, blk)] = flipped

        return carry

    lax.fori_loop(0, slots, put, 0)


def pair_up(a_ref, b_ref, out_ref):
    out_ref[0] = a_ref[...]
    out_ref[1] = b_ref[...]


def chosen_base(core_0_ref, core_1_ref, use):
    core = my_place()[1]

    @pl.when(core == 0)
    def _():
        use(core_0_ref)

    @pl.when(core != 0)
    def _():
        use(core_1_ref)


def join_base(pair_ref, hop_ref, g4_ref, out_ref):
    def put(ref):
        out_ref[:2] = ref[...]

    chosen_base(pair_ref, hop_ref, put)
    out_ref[2:] = g4_ref[...]


def join(a_ref, b_ref, out_ref):
    n = a_ref.shape[0]
    out_ref[:n] = a_ref[...]
    out_ref[n:] = b_ref[...]


def times(up_ref, first, *x_refs):
    parts = []
    for ref in x_refs:
        parts += [ref[n] for n in range(ref.shape[0])] if len(ref.shape) == 3 else [ref[...]]
    x = jnp.concatenate(parts, axis=1)
    feats = parts[0].shape[1]
    return jnp.dot(x, up_ref[first * feats : (first + len(parts)) * feats], preferred_element_type=F32)


def forward_first(x_ref, up_ref, out_ref):
    out_ref[...] = times(up_ref, 0, x_ref)


def forward_more(place, so_far, x_ref, up_ref, out_ref):
    out_ref[...] = so_far[...] + times(up_ref, place, x_ref)


def forward_last(so_far, x_ref, up_ref, og_ref, act_ref, pg_ref):
    hidden = so_far[...] + times(up_ref, 24, x_ref)
    sig = jax.nn.sigmoid(hidden)
    act_ref[...] = (hidden * sig).astype(BF16)
    pg_ref[...] = (og_ref[...].astype(F32) * sig * (1.0 + hidden * (1.0 - sig))).astype(BF16)


def back(first, pg_ref, pg2_ref, own_ref, sibling_ref, out_ref):
    for n in range(out_ref.shape[0]):
        out_ref[n] = (
            jnp.dot(pg_ref[...], own_ref[first + n], preferred_element_type=F32)
            + jnp.dot(pg2_ref[...], sibling_ref[first + n], preferred_element_type=F32)
        ).astype(out_ref.dtype)


def f32(v):
    return v.astype(F32)


def add_first(d_ref, r1_ref, out_ref):
    for n in range(4):
        out_ref[n] = (d_ref[4 + n] + f32(r1_ref[4 + n])).astype(BF16)


def add_second(d_ref, r1_ref, r2_ref, next_ref, base_ref):
    for n in range(2):
        base_ref[n] = (d_ref[n] + f32(r1_ref[n]) + f32(r2_ref[n])).astype(BF16)
        next_ref[n] = (d_ref[2 + n] + f32(r1_ref[2 + n]) + f32(r2_ref[2 + n])).astype(BF16)


def add_third(base_ref, hop_ref, r3_ref, cross_ref, own_ref):
    def put(ref):
        cross_ref[...] = (f32(ref[1]) + f32(r3_ref[1])).astype(BF16)
        own_ref[...] = f32(ref[0]) + f32(r3_ref[0])

    chosen_base(base_ref, hop_ref, put)


def add_last(own_ref, cross_ref, out_ref):
    out_ref[...] = (own_ref[...] + f32(cross_ref[...])).astype(BF16)


def weight_terms(listed_hbm, pg_ref, *refs):
    x_refs, (out_ref, listed, flipped, dense, sem) = refs[:-5], refs[-5:]
    fetch = pltpu.make_async_copy(listed_hbm, listed, sem)
    fetch.start()
    slots, blk = out_ref.shape[0], out_ref.shape[1]
    rows_per_dev = dense.shape[2] // blk
    me = my_place()
    flipped[...] = pg_ref[...].T
    for n, (ref, m) in enumerate([(ref, m) for ref in x_refs for m in range(ref.shape[0])]):
        dense[n] = jnp.dot(flipped[...], ref[m], preferred_element_type=F32).astype(BF16)

    fetch.wait()

    def one(s, carry):
        row, col = listed[0, s], listed[1, s]
        used = row >= 0
        row, col = jnp.maximum(row, 0), jnp.maximum(col, 0)
        mine, n = place_of(row // rows_per_dev, me)
        n = jnp.where(mine, n, n + NZ)
        block = dense[n, at(col, blk), at(lax.rem(row, rows_per_dev), blk)]
        out_ref[s] = jnp.where(used, block, jnp.zeros_like(block))
        return carry

    lax.fori_loop(0, slots, one, 0, unroll=4)


def add_terms(scale, in_ref, out_ref):
    for q in range(out_ref.shape[0]):
        total = f32(in_ref[0, q])
        for g in range(1, in_ref.shape[0]):
            total = total + f32(in_ref[g, q])
        out_ref[q] = total.T * scale


def kernel(body, out, ins=(), n_in=1, mib=16, flops=0, size=MIB, scratch=()):
    several = isinstance(out, tuple)
    return pl.pallas_call(
        body,
        out_shape=out,
        in_specs=list(ins) + [VMEM] * n_in,
        out_specs=(VMEM,) * len(out) if several else VMEM,
        scratch_shapes=scratch,
        compiler_params=params(mib),
        cost_estimate=cost(flops, size),
    )


def on_device(n_dp, tokens, up_blocks, block_list, row_cut, out_grad):
    tok_rows, feats = tokens.shape
    slots, blk = up_blocks.shape[1], up_blocks.shape[2]
    width = out_grad.shape[1]
    rows_per_dev = row_cut.shape[1]
    per = slots // n_dp
    listed, cut = block_list[0].T, row_cut.T
    around = range(NZ)
    together = lax.optimization_barrier

    def send(v, pairs):
        return lax.ppermute(v, "blk", pairs)

    def other_core(v):
        return send(v, [(n, n ^ 1) for n in range(2 * NZ)])

    def steps(v, d, d1=None):
        by = (d, -(d if d1 is None else d1))
        return send(v, [(2 * z + c, 2 * ((z + by[c]) % NZ) + c) for z in around for c in range(2)])

    def hop(v, d):
        return send(v, [(2 * z + 1, 2 * ((z + d) % NZ) + 1) for z in around])

    def flops_of(shards):
        return 2 * shards * tok_rows * feats * width

    def shards(n, dtype=BF16):
        return shape(n, tok_rows, feats, dtype=dtype)

    theirs = other_core(tokens)
    pair = kernel(pair_up, shards(2), n_in=2, size=0)(tokens, theirs)
    g4 = steps(pair, -4, -5)
    base = hop(pair, 1)
    pair, listed = together((pair, listed))
    up_w, down_w, down_other = kernel(
        lay_weights,
        (shape(2 * NZ * feats, width),) + (shape(NZ, width, feats),) * 2,
        ins=[HBM] * 3, n_in=0, mib=24, size=20 * MIB,
        scratch=[
            pltpu.SMEM(listed.shape, jnp.int32), pltpu.SMEM(cut.shape, jnp.int32), pltpu.SMEM((cut.size,), jnp.int32),
            pltpu.VMEM((slots, blk, blk), BF16), pltpu.SemaphoreType.DMA((3,)),
        ],
    )(in_hbm(listed), in_hbm(cut), in_hbm(up_blocks[0]))
    g4, up_w = together((g4, up_w))
    g04 = kernel(join_base, shards(4), n_in=3, size=0)(pair, base, g4)
    g26 = steps(g04, -2)
    early = kernel(join, shards(8), n_in=2, size=0)(g04, g26)
    late = steps(early, -1)
    early, down_other = together((early, down_other))
    early_other = other_core(early)
    down_sibling = other_core(down_other)

    hidden_shape = shape(tok_rows, width, dtype=F32)

    def more(body, *operands, flops=0):
        return kernel(body, hidden_shape, n_in=len(operands), flops=flops, size=0)(*operands)

    hidden = more(forward_first, early, up_w)
    late, hidden = together((late, hidden))
    late_other = other_core(late)
    hidden = more(functools.partial(forward_more, 8), hidden, late, up_w, flops=LONG)
    hidden = more(functools.partial(forward_more, 16), hidden, early_other, up_w)
    act, pg = kernel(forward_last, (shape(tok_rows, width),) * 2, n_in=4, flops=flops_of(4), size=4 * MIB)(
        hidden, late_other, up_w, out_grad
    )
    pg2 = other_core(pg)

    def back_of(first, dtype):
        return kernel(functools.partial(back, first), shards(8, dtype), n_in=4, flops=flops_of(8), size=4 * MIB)(
            pg, pg2, down_w, down_sibling
        )

    d1 = back_of(8, BF16)
    r1 = steps(d1, 1)
    pg, d1 = together((pg, d1))
    d2 = back_of(0, F32)
    pg, d2 = together((pg, d2))
    terms = kernel(
        weight_terms, shape(slots, blk, blk), ins=[HBM], n_in=5, mib=12,
        flops=flops_of(32), size=16 * MIB,
        scratch=[
            pltpu.SMEM(listed.shape, jnp.int32), pltpu.VMEM((width, tok_rows), BF16),
            pltpu.VMEM((2 * NZ, width, feats), BF16), pltpu.SemaphoreType.DMA,
        ],
    )(in_hbm(listed), pg, early, late, early_other, late_other)
    got = lax.all_to_all(terms, "dp", 0, 0, tiled=True)

    r2 = steps(kernel(add_first, shards(4), n_in=2, flops=FIRST, size=0)(d2, r1), 2)
    q, sums = kernel(add_second, (shards(2),) * 2, n_in=3, size=0)(d2, r1, r2)
    r3 = steps(q, 4, 5)
    moved = hop(sums, -1)
    own_grads = kernel(
        functools.partial(add_terms, 1.0 / (tok_rows * n_dp) ** 0.5), shape(per, blk, blk, dtype=F32), size=0
    )(got.reshape(n_dp, per, blk, blk))
    one = shape(tok_rows, feats)
    cross, total = kernel(add_third, (one, shape(tok_rows, feats, dtype=F32)), n_in=3, size=0)(sums, moved, r3)
    cross, own_grads = together((other_core(cross), own_grads))
    in_grad = kernel(add_last, one, n_in=2, size=0)(total, cross)
    return act, in_grad, own_grads[None]


def solution(mesh):
    return jax.shard_map(
        functools.partial(on_device, mesh.shape["dp"]),
        mesh=mesh,
        in_specs=(
            P("dp", "blk"),
            P("blk", None, None, None),
            P("blk", None, None),
            P(),
            P("dp", "blk"),
        ),
        out_specs=(P("dp", "blk"), P("dp", "blk"), P("blk", "dp", None, None)),
        check_vma=False,
    )
```

```python
import functools

import jax
import jax.numpy as jnp
from jax import lax
from jax.experimental import pallas as pl
from jax.experimental.pallas import tpu as pltpu
from jax.sharding import PartitionSpec as P

SMEM = pl.BlockSpec(memory_space=pltpu.SMEM)
VMEM = pl.BlockSpec(memory_space=pltpu.VMEM)
HBM = pl.BlockSpec(memory_space=pltpu.HBM)
MIB = 1 << 20
BF16, F32 = jnp.bfloat16, jnp.float32
NZ = 16
SET = 17
LONG = 80 * 10**9
FIRST = 200 * 10**9


def params(mib):
    return pltpu.CompilerParams(vmem_limit_bytes=mib * MIB)


def cost(flops, size):
    return pl.CostEstimate(flops=flops, bytes_accessed=size, transcendentals=0)


def shape(*dims, dtype=BF16):
    return jax.ShapeDtypeStruct(dims, dtype)


def my_place():
    here = lax.axis_index("blk")
    return here // 2, lax.rem(here, 2)


def place_of(dev, me):
    z, core = me
    step = lax.rem(dev // 2 - z + NZ, NZ)
    same = lax.rem(dev, 2) == core
    chosen = jnp.where(step == 0, core, (step > NZ // 2).astype(jnp.int32))
    i = jnp.where(step <= NZ // 2, step, NZ - step)
    second = (lax.rem(dev, 2) != chosen).astype(jnp.int32)
    place = 8 * lax.rem(i, 2) + 2 * (i // 4) + 4 * lax.rem(i // 2, 2) + second
    return step, same, chosen == core, jnp.where(step == NZ // 2, 16, place)


def up_place(dev, me):
    step, same, mine, n = place_of(dev, me)
    mine = jnp.where(step == NZ // 2, same.astype(jnp.int32), mine.astype(jnp.int32))
    return n + SET * (1 - mine)


def down_place(dev, me):
    step, same, mine, n = place_of(dev, me)
    by_parity = lax.rem(step, NZ // 2) == 0
    mine = jnp.where(by_parity, same.astype(jnp.int32), mine.astype(jnp.int32))
    return mine == 1, jnp.where(step == 0, 0, n)


def in_hbm(v):
    return pltpu.with_memory_space_constraint(v, pltpu.HBM)


def at(i, size):
    return pl.ds(pl.multiple_of(i * size, size), size)


def lay_weights(listed_hbm, cut_hbm, w_hbm, up_ref, own_ref, other_ref, listed, cut, place, w_ref, sems):
    copies = [
        pltpu.make_async_copy(src, dst, sems.at[n])
        for n, (src, dst) in enumerate(((listed_hbm, listed), (cut_hbm, cut), (w_hbm, w_ref)))
    ]
    for copy in copies:
        copy.start()
    slots, blk = w_ref.shape[0], w_ref.shape[1]
    rows_per_dev, devs = cut.shape
    me = my_place()

    def note(k, carry):
        for a in range(rows_per_dev):
            place[cut[a, k]] = k * rows_per_dev + a
        return carry

    for ref in (up_ref, own_ref, other_ref):
        ref[...] = jnp.zeros_like(ref)
    for copy in copies:
        copy.wait()
    lax.fori_loop(0, devs, note, 0)

    def put(s, carry):
        row, col = listed[0, s], listed[1, s]

        @pl.when(row >= 0)
        def _():
            block = w_ref[s]
            n = up_place(row // rows_per_dev, me)
            up_ref[at(n * rows_per_dev + lax.rem(row, rows_per_dev), blk), at(col, blk)] = block
            to = place[row]
            mine, n = down_place(to // rows_per_dev, me)
            a = lax.rem(to, rows_per_dev)
            flipped = block.T

            @pl.when(mine)
            def _():
                own_ref[n, at(col, blk), at(a, blk)] = flipped

            @pl.when(jnp.logical_not(mine))
            def _():
                other_ref[n, at(col, blk), at(a, blk)] = flipped

        return carry

    lax.fori_loop(0, slots, put, 0)


def pair_up(a_ref, b_ref, out_ref):
    out_ref[0] = a_ref[...]
    out_ref[1] = b_ref[...]


def join(a_ref, b_ref, out_ref):
    n = a_ref.shape[0]
    out_ref[:n] = a_ref[...]
    out_ref[n:] = b_ref[...]


def join_early(a_ref, b_ref, out_ref, sixth_ref):
    join(a_ref, b_ref, out_ref)
    sixth_ref[...] = b_ref[2]


def join_across(a_ref, b_ref, out_ref):
    out_ref[:8] = a_ref[...]
    out_ref[8] = b_ref[...]


def times(up_ref, first, *x_refs):
    parts = []
    for ref in x_refs:
        parts += [ref[n] for n in range(ref.shape[0])] if len(ref.shape) == 3 else [ref[...]]
    x = jnp.concatenate(parts, axis=1)
    feats = parts[0].shape[1]
    return jnp.dot(x, up_ref[first * feats : (first + len(parts)) * feats], preferred_element_type=F32)


def forward_first(x_ref, up_ref, out_ref):
    out_ref[...] = times(up_ref, 0, x_ref)


def forward_more(place, so_far, x_ref, up_ref, out_ref):
    out_ref[...] = so_far[...] + times(up_ref, place, x_ref)


def forward_last(so_far, x_ref, up_ref, og_ref, act_ref, pg_ref):
    hidden = so_far[...] + times(up_ref, 25, x_ref)
    sig = jax.nn.sigmoid(hidden)
    act_ref[...] = (hidden * sig).astype(BF16)
    pg_ref[...] = (og_ref[...].astype(F32) * sig * (1.0 + hidden * (1.0 - sig))).astype(BF16)


def back(first, pg_ref, pg2_ref, own_ref, sibling_ref, out_ref):
    for n in range(out_ref.shape[0]):
        out_ref[n] = (
            jnp.dot(pg_ref[...], own_ref[first + n], preferred_element_type=F32)
            + jnp.dot(pg2_ref[...], sibling_ref[first + n], preferred_element_type=F32)
        ).astype(out_ref.dtype)


def back_late(pg_ref, pg2_ref, own_ref, sibling_ref, out_ref, across_ref):
    back(8, pg_ref, pg2_ref, own_ref, sibling_ref, out_ref)
    across_ref[...] = (
        jnp.dot(pg_ref[...], own_ref[16], preferred_element_type=F32)
        + jnp.dot(pg2_ref[...], sibling_ref[16], preferred_element_type=F32)
    ).astype(BF16)


def f32(v):
    return v.astype(F32)


def add_first(d_ref, r1_ref, r8_ref, out_ref):
    for n in range(4):
        total = d_ref[4 + n] + f32(r1_ref[4 + n])
        out_ref[n] = (total + f32(r8_ref[...]) if n == 2 else total).astype(BF16)


def add_second(d_ref, r1_ref, r2_ref, next_ref, base_ref):
    for n in range(2):
        base_ref[n] = (d_ref[n] + f32(r1_ref[n]) + f32(r2_ref[n])).astype(BF16)
        next_ref[n] = (d_ref[2 + n] + f32(r1_ref[2 + n]) + f32(r2_ref[2 + n])).astype(BF16)


def add_third(base_ref, r3_ref, cross_ref, own_ref):
    cross_ref[...] = (f32(base_ref[1]) + f32(r3_ref[1])).astype(BF16)
    own_ref[...] = f32(base_ref[0]) + f32(r3_ref[0])


def add_last(own_ref, cross_ref, out_ref):
    out_ref[...] = (own_ref[...] + f32(cross_ref[...])).astype(BF16)


def weight_terms(listed_hbm, pg_ref, *refs):
    x_refs, (out_ref, listed, flipped, dense, sem) = refs[:-5], refs[-5:]
    fetch = pltpu.make_async_copy(listed_hbm, listed, sem)
    fetch.start()
    slots, blk = out_ref.shape[0], out_ref.shape[1]
    rows_per_dev = dense.shape[2] // blk
    me = my_place()
    flipped[...] = pg_ref[...].T
    for n, (ref, m) in enumerate([(ref, m) for ref in x_refs for m in range(ref.shape[0])]):
        dense[n] = jnp.dot(flipped[...], ref[m], preferred_element_type=F32).astype(BF16)

    fetch.wait()

    def one(s, carry):
        row, col = listed[0, s], listed[1, s]
        used = row >= 0
        row, col = jnp.maximum(row, 0), jnp.maximum(col, 0)
        n = up_place(row // rows_per_dev, me)
        block = dense[n, at(col, blk), at(lax.rem(row, rows_per_dev), blk)]
        out_ref[s] = jnp.where(used, block, jnp.zeros_like(block))
        return carry

    lax.fori_loop(0, slots, one, 0, unroll=4)


def add_terms(scale, in_ref, out_ref):
    for q in range(out_ref.shape[0]):
        total = f32(in_ref[0, q])
        for g in range(1, in_ref.shape[0]):
            total = total + f32(in_ref[g, q])
        out_ref[q] = total.T * scale


def kernel(body, out, ins=(), n_in=1, mib=16, flops=0, size=MIB, scratch=()):
    several = isinstance(out, tuple)
    return pl.pallas_call(
        body,
        out_shape=out,
        in_specs=list(ins) + [VMEM] * n_in,
        out_specs=(VMEM,) * len(out) if several else VMEM,
        scratch_shapes=scratch,
        compiler_params=params(mib),
        cost_estimate=cost(flops, size),
    )


def on_device(n_dp, tokens, up_blocks, block_list, row_cut, out_grad):
    tok_rows, feats = tokens.shape
    slots, blk = up_blocks.shape[1], up_blocks.shape[2]
    width = out_grad.shape[1]
    rows_per_dev = row_cut.shape[1]
    per = slots // n_dp
    listed, cut = block_list[0].T, row_cut.T
    around = range(NZ)
    together = lax.optimization_barrier

    def send(v, pairs):
        return lax.ppermute(v, "blk", pairs)

    def other_core(v):
        return send(v, [(n, n ^ 1) for n in range(2 * NZ)])

    def steps(v, d):
        return send(v, [(2 * z + c, 2 * ((z + (d, -d)[c]) % NZ) + c) for z in around for c in range(2)])

    def flops_of(shards):
        return 2 * shards * tok_rows * feats * width

    def shards(n, dtype=BF16):
        return shape(n, tok_rows, feats, dtype=dtype)

    theirs = other_core(tokens)
    pair = kernel(pair_up, shards(2), n_in=2, size=0)(tokens, theirs)
    g4 = steps(pair, -4)
    pair, listed = together((pair, listed))
    up_w, down_w, down_other = kernel(
        lay_weights,
        (shape(2 * SET * feats, width),) + (shape(SET, width, feats),) * 2,
        ins=[HBM] * 3, n_in=0, mib=24, size=20 * MIB,
        scratch=[
            pltpu.SMEM(listed.shape, jnp.int32), pltpu.SMEM(cut.shape, jnp.int32), pltpu.SMEM((cut.size,), jnp.int32),
            pltpu.VMEM((slots, blk, blk), BF16), pltpu.SemaphoreType.DMA((3,)),
        ],
    )(in_hbm(listed), in_hbm(cut), in_hbm(up_blocks[0]))
    g4, up_w = together((g4, up_w))
    g04 = kernel(join, shards(4), n_in=2, size=0)(pair, g4)
    g26 = steps(g04, -2)
    one = shape(tok_rows, feats)
    early, g6 = kernel(join_early, (shards(8), one), n_in=2, size=0)(g04, g26)
    late = steps(early, -1)
    g8 = steps(g6, -2)
    early, down_other = together((early, down_other))
    early_other = other_core(early)
    down_sibling = other_core(down_other)

    hidden_shape = shape(tok_rows, width, dtype=F32)

    def more(body, *operands, flops=0):
        return kernel(body, hidden_shape, n_in=len(operands), flops=flops, size=0)(*operands)

    hidden = more(forward_first, early, up_w)
    late, g8, hidden = together((late, g8, hidden))
    late = kernel(join_across, shards(9), n_in=2, size=0)(late, g8)
    late_other = other_core(late)
    hidden = more(functools.partial(forward_more, 8), hidden, late, up_w, flops=LONG)
    hidden = more(functools.partial(forward_more, 17), hidden, early_other, up_w)
    act, pg = kernel(forward_last, (shape(tok_rows, width),) * 2, n_in=4, flops=flops_of(4), size=4 * MIB)(
        hidden, late_other, up_w, out_grad
    )
    pg2 = other_core(pg)

    def back_of(first, dtype):
        return kernel(functools.partial(back, first), shards(8, dtype), n_in=4, flops=flops_of(8), size=4 * MIB)(
            pg, pg2, down_w, down_sibling
        )

    d1, d8 = kernel(back_late, (shards(8), one), n_in=4, flops=flops_of(9), size=4 * MIB)(pg, pg2, down_w, down_sibling)
    r1 = steps(d1, 1)
    r8 = steps(d8, 2)
    pg, d1 = together((pg, d1))
    d2 = back_of(0, F32)
    pg, d2 = together((pg, d2))
    terms = kernel(
        weight_terms, shape(slots, blk, blk), ins=[HBM], n_in=5, mib=12,
        flops=flops_of(32), size=16 * MIB,
        scratch=[
            pltpu.SMEM(listed.shape, jnp.int32), pltpu.VMEM((width, tok_rows), BF16),
            pltpu.VMEM((2 * SET, width, feats), BF16), pltpu.SemaphoreType.DMA,
        ],
    )(in_hbm(listed), pg, early, late, early_other, late_other)
    got = lax.all_to_all(terms, "dp", 0, 0, tiled=True)

    r2 = steps(kernel(add_first, shards(4), n_in=3, flops=FIRST, size=0)(d2, r1, r8), 2)
    q, sums = kernel(add_second, (shards(2),) * 2, n_in=3, size=0)(d2, r1, r2)
    r3 = steps(q, 4)
    own_grads = kernel(
        functools.partial(add_terms, 1.0 / (tok_rows * n_dp) ** 0.5), shape(per, blk, blk, dtype=F32), size=0
    )(got.reshape(n_dp, per, blk, blk))
    cross, total = kernel(add_third, (one, shape(tok_rows, feats, dtype=F32)), n_in=2, size=0)(sums, r3)
    cross, own_grads = together((other_core(cross), own_grads))
    in_grad = kernel(add_last, one, n_in=2, size=0)(total, cross)
    return act, in_grad, own_grads[None]


def solution(mesh):
    return jax.shard_map(
        functools.partial(on_device, mesh.shape["dp"]),
        mesh=mesh,
        in_specs=(
            P("dp", "blk"),
            P("blk", None, None, None),
            P("blk", None, None),
            P(),
            P("dp", "blk"),
        ),
        out_specs=(P("dp", "blk"), P("dp", "blk"), P("blk", "dp", None, None)),
        check_vma=False,
    )
```

```python
import functools

import jax
import jax.numpy as jnp
from jax import lax
from jax.experimental import pallas as pl
from jax.experimental.pallas import tpu as pltpu
from jax.sharding import PartitionSpec as P

SMEM = pl.BlockSpec(memory_space=pltpu.SMEM)
VMEM = pl.BlockSpec(memory_space=pltpu.VMEM)
HBM = pl.BlockSpec(memory_space=pltpu.HBM)
MIB = 1 << 20
BF16, F32 = jnp.bfloat16, jnp.float32
NZ = 16
LONG = 80 * 10**9
FIRST = 200 * 10**9


def params(mib):
    return pltpu.CompilerParams(vmem_limit_bytes=mib * MIB)


def cost(flops, size):
    return pl.CostEstimate(flops=flops, bytes_accessed=size, transcendentals=0)


def shape(*dims, dtype=BF16):
    return jax.ShapeDtypeStruct(dims, dtype)


def my_place():
    here = lax.axis_index("blk")
    return here // 2, lax.rem(here, 2)


def place_of(dev, me):
    z, core = me
    step = lax.rem(dev // 2 - z + NZ, NZ)
    chosen = (step >= NZ // 2).astype(jnp.int32)
    i = jnp.where(step < NZ // 2, step, NZ - 1 - step)
    second = (lax.rem(dev, 2) != chosen).astype(jnp.int32)
    return chosen == core, 8 * lax.rem(i, 2) + 2 * (i // 4) + 4 * lax.rem(i // 2, 2) + second


def in_hbm(v):
    return pltpu.with_memory_space_constraint(v, pltpu.HBM)


def at(i, size):
    return pl.ds(pl.multiple_of(i * size, size), size)


def lay_weights(listed_hbm, cut_hbm, w_hbm, up_ref, own_ref, other_ref, listed, cut, place, w_ref, sems):
    copies = [
        pltpu.make_async_copy(src, dst, sems.at[n])
        for n, (src, dst) in enumerate(((listed_hbm, listed), (cut_hbm, cut), (w_hbm, w_ref)))
    ]
    for copy in copies:
        copy.start()
    slots, blk = w_ref.shape[0], w_ref.shape[1]
    rows_per_dev, devs = cut.shape
    me = my_place()

    def note(k, carry):
        for a in range(rows_per_dev):
            place[cut[a, k]] = k * rows_per_dev + a
        return carry

    for ref in (up_ref, own_ref, other_ref):
        ref[...] = jnp.zeros_like(ref)
    for copy in copies:
        copy.wait()
    lax.fori_loop(0, devs, note, 0)

    def put(s, carry):
        row, col = listed[0, s], listed[1, s]

        @pl.when(row >= 0)
        def _():
            block = w_ref[s]
            mine, n = place_of(row // rows_per_dev, me)
            n = jnp.where(mine, n, n + NZ)
            up_ref[at(n * rows_per_dev + lax.rem(row, rows_per_dev), blk), at(col, blk)] = block
            to = place[row]
            mine, n = place_of(to // rows_per_dev, me)
            a = lax.rem(to, rows_per_dev)
            flipped = block.T

            @pl.when(mine)
            def _():
                own_ref[n, at(col, blk), at(a, blk)] = flipped

            @pl.when(jnp.logical_not(mine))
            def _():
                other_ref[n, at(col, blk), at(a, blk)] = flipped

        return carry

    lax.fori_loop(0, slots, put, 0)


def pair_up(a_ref, b_ref, out_ref):
    out_ref[0] = a_ref[...]
    out_ref[1] = b_ref[...]


def chosen_base(core_0_ref, core_1_ref, use):
    core = my_place()[1]

    @pl.when(core == 0)
    def _():
        use(core_0_ref)

    @pl.when(core != 0)
    def _():
        use(core_1_ref)


def join_base(pair_ref, hop_ref, g4_ref, out_ref):
    def put(ref):
        out_ref[:2] = ref[...]

    chosen_base(pair_ref, hop_ref, put)
    out_ref[2:] = g4_ref[...]


def join(a_ref, b_ref, out_ref):
    n = a_ref.shape[0]
    out_ref[:n] = a_ref[...]
    out_ref[n:] = b_ref[...]


def times(up_ref, first, *x_refs):
    parts = []
    for ref in x_refs:
        parts += [ref[n] for n in range(ref.shape[0])] if len(ref.shape) == 3 else [ref[...]]
    x = jnp.concatenate(parts, axis=1)
    feats = parts[0].shape[1]
    return jnp.dot(x, up_ref[first * feats : (first + len(parts)) * feats], preferred_element_type=F32)


def forward_first(x_ref, up_ref, out_ref):
    out_ref[...] = times(up_ref, 0, x_ref)


def forward_more(place, so_far, x_ref, up_ref, out_ref):
    out_ref[...] = so_far[...] + times(up_ref, place, x_ref)


def forward_last(so_far, x_ref, up_ref, og_ref, act_ref, pg_ref):
    hidden = so_far[...] + times(up_ref, 24, x_ref)
    sig = jax.nn.sigmoid(hidden)
    act_ref[...] = (hidden * sig).astype(BF16)
    pg_ref[...] = (og_ref[...].astype(F32) * sig * (1.0 + hidden * (1.0 - sig))).astype(BF16)


def back(first, pg_ref, pg2_ref, own_ref, sibling_ref, out_ref):
    for n in range(out_ref.shape[0]):
        out_ref[n] = (
            jnp.dot(pg_ref[...], own_ref[first + n], preferred_element_type=F32)
            + jnp.dot(pg2_ref[...], sibling_ref[first + n], preferred_element_type=F32)
        ).astype(out_ref.dtype)


def f32(v):
    return v.astype(F32)


def add_first(d_ref, r1_ref, out_ref):
    for n in range(4):
        out_ref[n] = (f32(d_ref[4 + n]) + f32(r1_ref[4 + n])).astype(BF16)


def add_second(d_ref, r1_ref, r2_ref, next_ref, base_ref):
    for n in range(2):
        base_ref[n] = (f32(d_ref[n]) + f32(r1_ref[n]) + f32(r2_ref[n])).astype(BF16)
        next_ref[n] = (f32(d_ref[2 + n]) + f32(r1_ref[2 + n]) + f32(r2_ref[2 + n])).astype(BF16)


def add_third(base_ref, hop_ref, r3_ref, cross_ref, own_ref):
    def put(ref):
        cross_ref[...] = (f32(ref[1]) + f32(r3_ref[1])).astype(BF16)
        own_ref[...] = f32(ref[0]) + f32(r3_ref[0])

    chosen_base(base_ref, hop_ref, put)


def add_last(own_ref, cross_ref, out_ref):
    out_ref[...] = (own_ref[...] + f32(cross_ref[...])).astype(BF16)


def weight_terms(listed_hbm, pg_ref, *refs):
    x_refs, (out_ref, listed, flipped, dense, sem) = refs[:-5], refs[-5:]
    fetch = pltpu.make_async_copy(listed_hbm, listed, sem)
    fetch.start()
    slots, blk = out_ref.shape[0], out_ref.shape[1]
    rows_per_dev = dense.shape[2] // blk
    me = my_place()
    flipped[...] = pg_ref[...].T
    for n, (ref, m) in enumerate([(ref, m) for ref in x_refs for m in range(ref.shape[0])]):
        dense[n] = jnp.dot(flipped[...], ref[m], preferred_element_type=F32).astype(BF16)

    fetch.wait()

    def one(s, carry):
        row, col = listed[0, s], listed[1, s]
        used = row >= 0
        row, col = jnp.maximum(row, 0), jnp.maximum(col, 0)
        mine, n = place_of(row // rows_per_dev, me)
        n = jnp.where(mine, n, n + NZ)
        block = dense[n, at(col, blk), at(lax.rem(row, rows_per_dev), blk)]
        out_ref[s] = jnp.where(used, block, jnp.zeros_like(block))
        return carry

    lax.fori_loop(0, slots, one, 0, unroll=4)


def add_terms(scale, in_ref, out_ref):
    for q in range(out_ref.shape[0]):
        total = f32(in_ref[0, q])
        for g in range(1, in_ref.shape[0]):
            total = total + f32(in_ref[g, q])
        out_ref[q] = total.T * scale


def kernel(body, out, ins=(), n_in=1, mib=16, flops=0, size=MIB, scratch=()):
    several = isinstance(out, tuple)
    return pl.pallas_call(
        body,
        out_shape=out,
        in_specs=list(ins) + [VMEM] * n_in,
        out_specs=(VMEM,) * len(out) if several else VMEM,
        scratch_shapes=scratch,
        compiler_params=params(mib),
        cost_estimate=cost(flops, size),
    )


def on_device(n_dp, tokens, up_blocks, block_list, row_cut, out_grad):
    tok_rows, feats = tokens.shape
    slots, blk = up_blocks.shape[1], up_blocks.shape[2]
    width = out_grad.shape[1]
    rows_per_dev = row_cut.shape[1]
    per = slots // n_dp
    listed, cut = block_list[0].T, row_cut.T
    around = range(NZ)
    together = lax.optimization_barrier

    def send(v, pairs):
        return lax.ppermute(v, "blk", pairs)

    def other_core(v):
        return send(v, [(n, n ^ 1) for n in range(2 * NZ)])

    def steps(v, d, d1=None):
        by = (d, -(d if d1 is None else d1))
        return send(v, [(2 * z + c, 2 * ((z + by[c]) % NZ) + c) for z in around for c in range(2)])

    def hop(v, d):
        return send(v, [(2 * z + 1, 2 * ((z + d) % NZ) + 1) for z in around])

    def flops_of(shards):
        return 2 * shards * tok_rows * feats * width

    def shards(n, dtype=BF16):
        return shape(n, tok_rows, feats, dtype=dtype)

    theirs = other_core(tokens)
    pair = kernel(pair_up, shards(2), n_in=2, size=0)(tokens, theirs)
    g4 = steps(pair, -4, -5)
    base = hop(pair, 1)
    pair, listed = together((pair, listed))
    up_w, down_w, down_other = kernel(
        lay_weights,
        (shape(2 * NZ * feats, width),) + (shape(NZ, width, feats),) * 2,
        ins=[HBM] * 3, n_in=0, mib=24, size=20 * MIB,
        scratch=[
            pltpu.SMEM(listed.shape, jnp.int32), pltpu.SMEM(cut.shape, jnp.int32), pltpu.SMEM((cut.size,), jnp.int32),
            pltpu.VMEM((slots, blk, blk), BF16), pltpu.SemaphoreType.DMA((3,)),
        ],
    )(in_hbm(listed), in_hbm(cut), in_hbm(up_blocks[0]))
    g4, up_w = together((g4, up_w))
    g04 = kernel(join_base, shards(4), n_in=3, size=0)(pair, base, g4)
    g26 = steps(g04, -2)
    early = kernel(join, shards(8), n_in=2, size=0)(g04, g26)
    late = steps(early, -1)
    early, down_other = together((early, down_other))
    early_other = other_core(early)
    down_sibling = other_core(down_other)

    hidden_shape = shape(tok_rows, width, dtype=F32)

    def more(body, *operands, flops=0):
        return kernel(body, hidden_shape, n_in=len(operands), flops=flops, size=0)(*operands)

    hidden = more(forward_first, early, up_w)
    late, hidden = together((late, hidden))
    late_other = other_core(late)
    hidden = more(functools.partial(forward_more, 8), hidden, late, up_w, flops=LONG)
    hidden = more(functools.partial(forward_more, 16), hidden, early_other, up_w)
    act, pg = kernel(forward_last, (shape(tok_rows, width),) * 2, n_in=4, flops=flops_of(4), size=4 * MIB)(
        hidden, late_other, up_w, out_grad
    )
    pg2 = other_core(pg)

    def back_of(first, dtype):
        return kernel(functools.partial(back, first), shards(8, dtype), n_in=4, flops=flops_of(8), size=4 * MIB)(
            pg, pg2, down_w, down_sibling
        )

    d1 = back_of(8, BF16)
    r1 = steps(d1, 1)
    pg, d1 = together((pg, d1))
    d2 = back_of(0, BF16)
    pg, d2 = together((pg, d2))
    terms = kernel(
        weight_terms, shape(slots, blk, blk), ins=[HBM], n_in=5, mib=14,
        flops=flops_of(32), size=16 * MIB,
        scratch=[
            pltpu.SMEM(listed.shape, jnp.int32), pltpu.VMEM((width, tok_rows), BF16),
            pltpu.VMEM((2 * NZ, width, feats), BF16), pltpu.SemaphoreType.DMA,
        ],
    )(in_hbm(listed), pg, early, late, early_other, late_other)
    got = lax.all_to_all(terms, "dp", 0, 0, tiled=True)

    r2 = steps(kernel(add_first, shards(4), n_in=2, flops=FIRST, size=0)(d2, r1), 2)
    q, sums = kernel(add_second, (shards(2),) * 2, n_in=3, size=0)(d2, r1, r2)
    r3 = steps(q, 4, 5)
    moved = hop(sums, -1)
    own_grads = kernel(
        functools.partial(add_terms, 1.0 / (tok_rows * n_dp) ** 0.5), shape(per, blk, blk, dtype=F32), size=0
    )(got.reshape(n_dp, per, blk, blk))
    r3, moved, own_grads = together((r3, moved, own_grads))
    one = shape(tok_rows, feats)
    cross, total = kernel(add_third, (one, shape(tok_rows, feats, dtype=F32)), n_in=3, size=0)(sums, moved, r3)
    in_grad = kernel(add_last, one, n_in=2, size=0)(total, other_core(cross))
    return act, in_grad, own_grads[None]


def solution(mesh):
    return jax.shard_map(
        functools.partial(on_device, mesh.shape["dp"]),
        mesh=mesh,
        in_specs=(
            P("dp", "blk"),
            P("blk", None, None, None),
            P("blk", None, None),
            P(),
            P("dp", "blk"),
        ),
        out_specs=(P("dp", "blk"), P("dp", "blk"), P("blk", "dp", None, None)),
        check_vma=False,
    )
```
